256 devices in a mesh: row: 64 (over z, x, core), col: 4 (over y).
Axes of the slice: x: 4, y: 4, z: 8, core: 2. Of those that a mesh axis runs over, the one named last changes fastest.
Arguments:
- tile_values: bfloat16 [64, 4, 360, 128, 128], P('row', 'col')
- tile_places: int32 [64, 4, 2, 360], P('row', 'col'), may hold values from 0 to 383, as said below
- tile_counts: int32 [64, 4], P('row', 'col'), may hold values from 90 to 360, as said below
- sketch: bfloat16 [196608, 512], P('col'), may hold values from -6 to 6
Outputs:
- range_basis: float32 [196608, 512], P(('row', 'col'))
- triangle: float32 [512, 512], replicated
The draws below stay inside these ranges and needn't reach their ends.
Inputs may be any that keep to these rules, and one draw needn't show every extreme that they name: `tile_places`: entry [r, c, 0, t] is the slot's tile row among the 24 tile rows of row block r and entry [r, c, 1, t] its tile column among the 384 tile columns of column block c; the 360 slots of one block pair name distinct positions, padded slots included. Slots t < tile_counts[r, c] hold the live tiles of block pair (r, c); later slots are padding and contribute nothing. Some block pair holds exactly 360 live tiles.
All inputs are finite; a program needn't handle non-finite values.
Results may differ from the reference program's by a relative error of at most 0.0003.
Values sent between devices are 32-bit elements; how exact they have to be, the bound alone decides.
A program may use at most 192 MiB of HBM per device.

```python
import math
import jax
import jax.numpy as jnp
from jax import lax

TILE = 128
K = 512
TMAX = 360
ROW_BLOCKS = 64
COL_BLOCKS = 4
TROWS = 24
TCOLS = 384
NORDER = 196608


def draw_tile_values(key, part):
    keys = jax.random.split(key, 2)
    full_shape = (ROW_BLOCKS, COL_BLOCKS, TMAX, TILE, TILE)
    entries = jax.random.normal(keys[0], full_shape, jnp.float32)
    growth = 3.0
    row_spread = jnp.exp(jax.random.uniform(keys[1], (ROW_BLOCKS, COL_BLOCKS, TMAX, TILE, 1), jnp.float32, -1.15, 1.15))
    block_growth = growth ** (jnp.arange(ROW_BLOCKS, dtype=jnp.float32) / max(ROW_BLOCKS - 1, 1))
    fan_total = TILE * (COL_BLOCKS * TMAX // (2 * TROWS) + 1)
    values = entries * row_spread * (block_growth[:, None, None, None, None] / math.sqrt(fan_total))
    return values.astype(jnp.bfloat16)


def draw_tile_places(key, part):
    keys = jax.random.split(key, ROW_BLOCKS * COL_BLOCKS)

    def pick_slots(one_key):
        return jax.random.permutation(one_key, TROWS * TCOLS)[:TMAX].astype(jnp.int32)
    chosen = jax.vmap(pick_slots)(keys).reshape(ROW_BLOCKS, COL_BLOCKS, TMAX)
    return jnp.stack([chosen // TCOLS, chosen % TCOLS], axis=2).astype(jnp.int32)


def draw_tile_counts(key, part):
    keys = jax.random.split(key, 2)
    low_count = TMAX // 4
    span_count = TMAX - low_count
    raw_draw = jax.random.randint(keys[0], (ROW_BLOCKS * COL_BLOCKS,), 0, span_count + 1, dtype=jnp.int32)
    counted = low_count + raw_draw * raw_draw // span_count
    busiest = jax.random.randint(keys[1], (), 0, ROW_BLOCKS * COL_BLOCKS, dtype=jnp.int32)
    counted = counted.at[busiest].set(TMAX)
    return counted.reshape(ROW_BLOCKS, COL_BLOCKS).astype(jnp.int32)


def shard_levels(own_key, dims, shards, least, largest):
    level, own = 1.0, jax.random.fold_in(own_key, 6)
    for dim, shards_of in shards:
        steps = jnp.exp(jax.random.uniform(jax.random.fold_in(own, dim), (shards_of,), jnp.float32, least / len(shards), largest / len(shards)))
        level = level * jnp.repeat(steps, dims[dim] // shards_of).reshape([-1 if axis == dim else 1 for axis in range(len(dims))])
    return level


def bell_draw(rng, extent, scale, reach, pieces=(), held_as=jnp.bfloat16):
    gain = shard_levels(rng, extent, pieces, -0.22, 0.18) if pieces else 1.0
    result = jax.random.normal(rng, extent, jnp.float32) * scale * gain
    return jnp.minimum(jnp.maximum(result, -reach), reach).astype(held_as)


def setup_inputs(seed: int = 0) -> dict:
    streams_of = jax.random.split(jax.random.key(seed), 5)
    return {
        "tile_values": draw_tile_values(jax.random.fold_in(streams_of[4], 71), 0),
        "tile_places": draw_tile_places(jax.random.fold_in(streams_of[4], 71), 0),
        "tile_counts": draw_tile_counts(jax.random.fold_in(streams_of[4], 71), 0),
        "sketch": bell_draw(streams_of[3], (NORDER, K), 1.0, 6.0, ((0, 4),)),
    }


def reference(tile_values, tile_places, tile_counts, sketch):
    panels = sketch.reshape(COL_BLOCKS, TCOLS, TILE, K)

    def row_block(block_row):

        def add_column(partial_value, block_col):
            tile_stack = tile_values[block_row, block_col]
            places = tile_places[block_row, block_col]
            live_mask = jnp.arange(TMAX, dtype=jnp.int32) < tile_counts[block_row, block_col]
            picked = panels[block_col][places[1]]
            products = jnp.einsum('tab,tbk->tak', tile_stack.astype(jnp.float32), picked.astype(jnp.float32), precision=lax.Precision.HIGHEST)
            products = jnp.where(live_mask[:, None, None], products, jnp.zeros_like(products))
            return (partial_value + jax.ops.segment_sum(products, places[0], num_segments=TROWS), None)
        partial_value, unused = lax.scan(add_column, jnp.zeros((TROWS, TILE, K), jnp.float32), jnp.arange(COL_BLOCKS, dtype=jnp.int32))
        return partial_value.reshape(TROWS * TILE, K)
    sketched = lax.map(row_block, jnp.arange(ROW_BLOCKS, dtype=jnp.int32)).reshape(NORDER, K)
    gram = jnp.dot(sketched.T.astype(jnp.float32), sketched.astype(jnp.float32), precision=lax.Precision.HIGHEST, preferred_element_type=jnp.float32)
    lower = jnp.linalg.cholesky(gram)
    order_scale = jnp.sqrt(jnp.float32(NORDER))
    basis_t = jax.scipy.linalg.solve_triangular(lower, sketched.T, lower=True)
    return (basis_t.T * order_scale, lower.T / order_scale)
```

```python
import functools, math
import jax
import jax.numpy as jnp
from jax import lax
from jax.experimental import pallas as pl
from jax.experimental.pallas import tpu as pltpu
from jax.sharding import PartitionSpec as P

GROUP = 4
TURN = 3
RING = 12

def sparse_kernel(base, plan_ref, span_ref, tiles, panels, *rest):
    nout = len(rest) - 6
    outs = rest[:nout]
    lhs, rhs, sums, tsem, psem, osem = rest[nout:]
    first = span_ref[0]
    last = span_ref[1]
    size = tiles.shape[1]
    rows_each = outs[0].shape[0]
    spare = nout * rows_each

    def parts(g, k):
        word = plan_ref[g * GROUP + k]
        s = lax.rem(g, RING)
        live = word >= (1 << 23)
        tile = pltpu.make_async_copy(tiles.at[word & 511], lhs.at[s, :, pl.ds(k * size, size)], tsem.at[s, k])
        panel = pltpu.make_async_copy(panels.at[(word >> 9) & 511], rhs.at[s, pl.ds(k * size, size), :], psem.at[s, k])
        return live, tile, panel, s

    def issue(g):
        for k in range(GROUP):
            live, tile, panel, s = parts(g, k)
            @pl.when(live)
            def _():
                tile.start()
                panel.start()
            if k:
                @pl.when(jnp.logical_not(live))
                def _():
                    lhs[s, :, k * size:(k + 1) * size] = jnp.zeros((size, size), lhs.dtype)
                    rhs[s, k * size:(k + 1) * size, :] = jnp.zeros((size, rhs.shape[2]), rhs.dtype)

    def prime(g, c):
        issue(g)
        return c

    lax.fori_loop(first, jnp.minimum(first + RING - TURN, last), prime, 0)

    def clear(i, c):
        sums[i] = jnp.zeros(sums.shape[1:], sums.dtype)
        return c

    lax.fori_loop(0, sums.shape[0], clear, 0)

    def step(turn, carry):
        g0 = first + turn * TURN
        for u in range(TURN):
            g = g0 + u
            @pl.when(g + RING - TURN < last)
            def _():
                issue(g + RING - TURN)
            @pl.when(g < last)
            def _():
                for k in range(GROUP):
                    live, tile, panel, s = parts(g, k)
                    @pl.when(live)
                    def _():
                        tile.wait()
                        panel.wait()
        for u in range(TURN):
            g = g0 + u
            s = lax.rem(g, RING)
            place = jnp.where(g < last, ((plan_ref[jnp.minimum(g, last - 1) * GROUP] >> 18) & 31) - base, spare)
            prod = jnp.dot(lhs[s], rhs[s], preferred_element_type=jnp.float32)
            sums[place] = sums[place] + prod
        return carry

    lax.fori_loop(0, lax.div(last - first + TURN - 1, TURN), step, 0)
    copies = [pltpu.make_async_copy(sums.at[pl.ds(i * rows_each, rows_each)], o, osem.at[i]) for i, o in enumerate(outs)]
    for c in copies:
        c.start()
    for c in copies:
        c.wait()

def sparse_sum(plan, span, tiles, panels, base, shape):
    nout, rows = shape
    width = panels.shape[2]
    size = tiles.shape[1]
    return pl.pallas_call(
        functools.partial(sparse_kernel, base),
        grid_spec=pltpu.PrefetchScalarGridSpec(
            num_scalar_prefetch=2, grid=(),
            in_specs=[pl.BlockSpec(memory_space=pl.ANY)] * 2,
            out_specs=[pl.BlockSpec(memory_space=pl.ANY)] * nout,
            scratch_shapes=[pltpu.VMEM((RING, size, GROUP * size), tiles.dtype), pltpu.VMEM((RING, GROUP * size, width), panels.dtype),
                            pltpu.VMEM((nout * rows + 1, size, width), jnp.float32),
                            pltpu.SemaphoreType.DMA((RING, GROUP)), pltpu.SemaphoreType.DMA((RING, GROUP)), pltpu.SemaphoreType.DMA((nout,))]),
        out_shape=[jax.ShapeDtypeStruct((rows, size, width), jnp.float32)] * nout,
        compiler_params=pltpu.CompilerParams(vmem_limit_bytes=40 << 20),
        cost_estimate=pl.CostEstimate(flops=2 * 360 * 128 * 128 * 512 * rows * nout // 24, bytes_accessed=50_000_000 * rows * nout // 24, transcendentals=0),
        name="tile_sums",
    )(plan, span, tiles, panels)

def make_plan(places, count, me, ncol, chunk_rows):
    rows = places[0]
    cols = places[1]
    n = rows.shape[0]
    nplace = ncol * chunk_rows
    ids = jnp.arange(n, dtype=jnp.int32)
    half = chunk_rows // 2
    dest = rows // chunk_rows
    sub = rows % chunk_rows
    step = jnp.where(sub < half, (me - 1 - dest) % ncol, (dest - 1 - me) % ncol)
    live = ids < count
    place = jnp.where(live, step * chunk_rows + sub, nplace)
    rank = jnp.sum(((place[None, :] == place[:, None]) & (ids[None, :] < ids[:, None])).astype(jnp.int32), axis=1)
    which = jnp.arange(nplace, dtype=jnp.int32)
    held = jnp.sum((place[None, :] == which[:, None]).astype(jnp.int32), axis=1)
    groups = (held + GROUP - 1) // GROUP
    ahead = jnp.sum(jnp.where(which[None, :] < place[:, None], groups[None, :], 0), axis=1)
    spot = jnp.where(live, ahead * GROUP + rank, -1)
    word = ids | (cols << 9) | (place << 18) | (1 << 23)
    total = -(-(n // GROUP + nplace) * GROUP // 128) * 128
    plan = jnp.sum(jnp.where(spot[None, :] == jnp.arange(total, dtype=jnp.int32)[:, None], word[None, :], 0), axis=1)
    n0 = jnp.sum(jnp.where(which < chunk_rows, groups, 0))
    n1 = jnp.sum(groups)
    return plan, jnp.stack([jnp.int32(0), n0]), jnp.stack([n0, n1])


HI = lax.Precision.HIGHEST

def dot_hi(a, b, dims):
    return lax.dot_general(a, b, (dims, ((), ())), precision=HI, preferred_element_type=jnp.float32)

def factor_block(a_ref, w_ref, u_ref, m):
    n = 128
    nv = n // 8
    lane = lax.broadcasted_iota(jnp.int32, (8, n), 1)
    sub = lax.broadcasted_iota(jnp.int32, (8, n), 0)
    a = [a_ref[8 * v:8 * v + 8, :] for v in range(nv)]
    b = [jnp.where(lane == sub + 8 * v, 1.0, 0.0).astype(jnp.float32) for v in range(nv)]
    for r in range(nv):
        col = {}
        for v in range(r, nv):
            for k in range(8):
                col[k, v] = jnp.broadcast_to(a[v][:, 8 * r + k:8 * r + k + 1], (8, n))
        e = {}
        for k in range(8):
            for j in range(k, 8):
                e[k, j] = jnp.broadcast_to(col[j, r][k:k + 1, :], (8, n))
        ra = [jnp.broadcast_to(a[r][k:k + 1, :], (8, n)) for k in range(8)]
        rb = [jnp.broadcast_to(b[r][k:k + 1, :], (8, n)) for k in range(8)]
        for k in range(8):
            rs = lax.rsqrt(e[k, k])
            for j in range(k + 1, 8):
                e[k, j] = e[k, j] * rs
            for i in range(k + 1, 8):
                for j in range(i, 8):
                    e[i, j] = e[i, j] - e[k, i] * e[k, j]
            ra[k] = ra[k] * rs
            rb[k] = rb[k] * rs
            for j in range(k + 1, 8):
                ra[j] = ra[j] - e[k, j] * ra[k]
                rb[j] = rb[j] - e[k, j] * rb[k]
            for v in range(r + 1, nv):
                col[k, v] = col[k, v] * rs
                for j in range(k + 1, 8):
                    col[j, v] = col[j, v] - e[k, j] * col[k, v]
                a[v] = a[v] - col[k, v] * ra[k]
                b[v] = b[v] - col[k, v] * rb[k]
        ua, ub = ra[0], rb[0]
        for k in range(1, 8):
            ua = jnp.where(sub == k, ra[k], ua)
            ub = jnp.where(sub == k, rb[k], ub)
        u_ref[8 * r:8 * r + 8, :] = jnp.where(lane >= sub + 8 * r, ua, 0.0)
        w_ref[8 * r:8 * r + 8, :] = ub

def chol_kernel(scale, g_ref, s_ref, x_ref, t_ref, gw, xs, d_ref, w_ref, u_ref):
    n = g_ref.shape[0]
    nb = n // 128
    gw[...] = g_ref[...]
    xs[...] = s_ref[...] * scale
    t_ref[...] = jnp.zeros_like(t_ref)
    for k in range(nb):
        lo = 128 * k
        hi = lo + 128
        d_ref[...] = gw[lo:hi, lo:hi]
        factor_block(d_ref, w_ref, u_ref, k)
        w = w_ref[...]
        t_ref[lo:hi, lo:hi] = u_ref[...] * (1.0 / scale)
        xk = dot_hi(xs[:, lo:hi], w, ((1,), (1,)))
        x_ref[:, lo:hi] = xk
        if hi < n:
            up = dot_hi(w, gw[lo:hi, hi:n], ((1,), (0,)))
            t_ref[lo:hi, hi:n] = up * (1.0 / scale)
            gw[hi:n, hi:n] = gw[hi:n, hi:n] - dot_hi(up, up, ((0,), (0,)))
            xs[:, hi:n] = xs[:, hi:n] - dot_hi(xk, up, ((1,), (0,)))

def chol_solve(gram, rows, scale):
    m, n = rows.shape
    return pl.pallas_call(
        functools.partial(chol_kernel, scale),
        out_shape=(jax.ShapeDtypeStruct((m, n), jnp.float32), jax.ShapeDtypeStruct((n, n), jnp.float32)),
        in_specs=[pl.BlockSpec(memory_space=pltpu.VMEM)] * 2,
        out_specs=(pl.BlockSpec(memory_space=pltpu.VMEM),) * 2,
        scratch_shapes=[pltpu.VMEM((n, n), jnp.float32), pltpu.VMEM((m, n), jnp.float32),
                        pltpu.VMEM((128, 128), jnp.float32), pltpu.VMEM((128, 128), jnp.float32),
                        pltpu.VMEM((128, 128), jnp.float32)],
        name="factor_solve",
    )(gram, rows)


def shifted(block, distance):
    count = lax.axis_size("col")
    return lax.ppermute(block, "col", [(i, (i + distance) % count) for i in range(count)])


def body(tile_values, tile_places, tile_counts, sketch):
    tile_stack = tile_values[0, 0]
    tile_size = tile_stack.shape[1]
    sketch_width = sketch.shape[1]
    row_devices = lax.axis_size("row")
    col_devices = lax.axis_size("col")
    local_rows = sketch.shape[0] // row_devices
    chunk_rows = local_rows // tile_size
    half = chunk_rows // 2
    panels = sketch.reshape(-1, tile_size, sketch_width)
    me = lax.axis_index("col")
    plan, span0, span1 = make_plan(tile_places[0, 0], tile_counts[0, 0], me, col_devices, chunk_rows)
    up, down = sparse_sum(plan, span0, tile_stack, panels, 0, (2, half))
    later = sparse_sum(plan, span1, tile_stack, panels, chunk_rows, (2 * (col_devices - 1), half))
    for turn in range(col_devices - 1):
        up = shifted(up, 1) + later[2 * turn]
        down = shifted(down, -1) + later[2 * turn + 1]
    own_rows = jnp.concatenate([up, down], axis=0).reshape(local_rows, sketch_width)
    gram_local = jnp.dot(own_rows.T, own_rows, precision=HI, preferred_element_type=jnp.float32)
    gram_whole = lax.psum(gram_local, ("row", "col"))
    order_scale = math.sqrt(local_rows * row_devices * col_devices)
    basis_rows, upper = chol_solve(gram_whole, own_rows, order_scale)
    return basis_rows, upper


def solution(mesh):
    in_specs = (
        P("row", "col", None, None, None),
        P("row", "col", None, None),
        P("row", "col"),
        P("col", None),
    )
    out_specs = (P(("row", "col"), None), P())
    return jax.shard_map(body, mesh=mesh, in_specs=in_specs, out_specs=out_specs, check_vma=False)
```

```python
import functools, math
import jax
import jax.numpy as jnp
from jax import lax
from jax.experimental import pallas as pl
from jax.experimental.pallas import tpu as pltpu
from jax.sharding import PartitionSpec as P

GROUP = 4
TURN = 3
RING = 12

def sparse_kernel(base, plan_ref, span_ref, tiles, panels, *rest):
    nout = len(rest) - 6
    outs = rest[:nout]
    lhs, rhs, sums, tsem, psem, osem = rest[nout:]
    first = span_ref[0]
    last = span_ref[1]
    size = tiles.shape[1]
    rows_each = outs[0].shape[0]
    spare = nout * rows_each

    def parts(g, k):
        word = plan_ref[g * GROUP + k]
        s = lax.rem(g, RING)
        live = word >= (1 << 23)
        tile = pltpu.make_async_copy(tiles.at[word & 511], lhs.at[s, :, pl.ds(k * size, size)], tsem.at[s, k])
        panel = pltpu.make_async_copy(panels.at[(word >> 9) & 511], rhs.at[s, pl.ds(k * size, size), :], psem.at[s, k])
        return live, tile, panel, s

    def issue(g):
        for k in range(GROUP):
            live, tile, panel, s = parts(g, k)
            @pl.when(live)
            def _():
                tile.start()
                panel.start()
            if k:
                @pl.when(jnp.logical_not(live))
                def _():
                    lhs[s, :, k * size:(k + 1) * size] = jnp.zeros((size, size), lhs.dtype)
                    rhs[s, k * size:(k + 1) * size, :] = jnp.zeros((size, rhs.shape[2]), rhs.dtype)

    def prime(g, c):
        issue(g)
        return c

    lax.fori_loop(first, jnp.minimum(first + RING - TURN, last), prime, 0)

    def clear(i, c):
        sums[i] = jnp.zeros(sums.shape[1:], sums.dtype)
        return c

    lax.fori_loop(0, sums.shape[0], clear, 0)

    def step(turn, carry):
        g0 = first + turn * TURN
        for u in range(TURN):
            g = g0 + u
            @pl.when(g + RING - TURN < last)
            def _():
                issue(g + RING - TURN)
            @pl.when(g < last)
            def _():
                for k in range(GROUP):
                    live, tile, panel, s = parts(g, k)
                    @pl.when(live)
                    def _():
                        tile.wait()
                        panel.wait()
        for u in range(TURN):
            g = g0 + u
            s = lax.rem(g, RING)
            place = jnp.where(g < last, ((plan_ref[jnp.minimum(g, last - 1) * GROUP] >> 18) & 31) - base, spare)
            prod = jnp.dot(lhs[s], rhs[s], preferred_element_type=jnp.float32)
            sums[place] = sums[place] + prod
        return carry

    lax.fori_loop(0, lax.div(last - first + TURN - 1, TURN), step, 0)
    copies = [pltpu.make_async_copy(sums.at[pl.ds(i * rows_each, rows_each)], o, osem.at[i]) for i, o in enumerate(outs)]
    for c in copies:
        c.start()
    for c in copies:
        c.wait()

def sparse_sum(plan, span, tiles, panels, base, shape):
    nout, rows = shape
    width = panels.shape[2]
    size = tiles.shape[1]
    return pl.pallas_call(
        functools.partial(sparse_kernel, base),
        grid_spec=pltpu.PrefetchScalarGridSpec(
            num_scalar_prefetch=2, grid=(),
            in_specs=[pl.BlockSpec(memory_space=pl.ANY)] * 2,
            out_specs=[pl.BlockSpec(memory_space=pl.ANY)] * nout,
            scratch_shapes=[pltpu.VMEM((RING, size, GROUP * size), tiles.dtype), pltpu.VMEM((RING, GROUP * size, width), panels.dtype),
                            pltpu.VMEM((nout * rows + 1, size, width), jnp.float32),
                            pltpu.SemaphoreType.DMA((RING, GROUP)), pltpu.SemaphoreType.DMA((RING, GROUP)), pltpu.SemaphoreType.DMA((nout,))]),
        out_shape=[jax.ShapeDtypeStruct((rows, size, width), jnp.float32)] * nout,
        compiler_params=pltpu.CompilerParams(vmem_limit_bytes=60 << 20),
        cost_estimate=pl.CostEstimate(flops=2 * 360 * 128 * 128 * 512 * rows * nout // 24, bytes_accessed=50_000_000 * rows * nout // 24, transcendentals=0),
        name="tile_sums",
    )(plan, span, tiles, panels)

def make_plan(places, count, me, ncol, chunk_rows):
    rows = places[0]
    cols = places[1]
    n = rows.shape[0]
    nplace = ncol * chunk_rows
    ids = jnp.arange(n, dtype=jnp.int32)
    half = chunk_rows // 2
    dest = rows // chunk_rows
    sub = rows % chunk_rows
    step = jnp.where(sub < half, (me - 1 - dest) % ncol, (dest - 1 - me) % ncol)
    live = ids < count
    place = jnp.where(live, step * chunk_rows + sub, nplace)
    rank = jnp.sum(((place[None, :] == place[:, None]) & (ids[None, :] < ids[:, None])).astype(jnp.int32), axis=1)
    which = jnp.arange(nplace, dtype=jnp.int32)
    held = jnp.sum((place[None, :] == which[:, None]).astype(jnp.int32), axis=1)
    groups = (held + GROUP - 1) // GROUP
    ahead = jnp.sum(jnp.where(which[None, :] < place[:, None], groups[None, :], 0), axis=1)
    spot = jnp.where(live, ahead * GROUP + rank, -1)
    word = ids | (cols << 9) | (place << 18) | (1 << 23)
    total = -(-(n // GROUP + nplace) * GROUP // 128) * 128
    plan = jnp.sum(jnp.where(spot[None, :] == jnp.arange(total, dtype=jnp.int32)[:, None], word[None, :], 0), axis=1)
    n0 = jnp.sum(jnp.where(which < chunk_rows, groups, 0))
    n1 = jnp.sum(groups)
    return plan, jnp.stack([jnp.int32(0), n0]), jnp.stack([n0, n1])


HI = lax.Precision.HIGHEST

def dot_hi(a, b, dims):
    return lax.dot_general(a, b, (dims, ((), ())), precision=HI, preferred_element_type=jnp.float32)

MESH = pl.DeviceIdType.MESH
HALF = ((0, 1, 0, 1), (2, 1, 2, 1), (0, 1, 1, 1), (2, -2, 3, 0), (0, 1, 2, 1))

def gram_kernel(dims, rows_ref, out_ref, part, mate, mine, inbox, tower, full, cs, cr, ps, pr, zs, zr, gs, gr, fs, fr):
    zn, xn, yn = dims
    row = lax.axis_index("row")
    y = lax.axis_index("col")
    core = lax.rem(row, 2)
    x = lax.rem(row // 2, xn)
    z = row // (2 * xn)
    other = 1 - core

    def at(zz, xx, yy, cc):
        return ((zz * xn + xx) * 2 + cc, yy)

    partner = at(z, x, y, other)
    plane = []
    for j in range(1, xn * yn):
        dx, dy = j // yn, j % yn
        plane.append((at(z, lax.rem(x + dx, xn), lax.rem(y + dy, yn), core),
                      lax.rem(x + dx, xn) * yn + lax.rem(y + dy, yn),
                      lax.rem(x + xn - dx, xn) * yn + lax.rem(y + yn - dy, yn)))
    column = [at(lax.rem(z + j, zn), x, y, core) for j in range(1, zn)]
    own = x * yn + y
    piece = mine.shape[0] // (xn * yn)

    barrier = pltpu.get_barrier_semaphore()
    peers = [partner] + [p[0] for p in plane] + column
    for peer in peers:
        pl.semaphore_signal(barrier, inc=1, device_id=peer, device_id_type=MESH)

    def fill(h):
        for b, (i0, i1, j0, j1) in enumerate(HALF):
            left = rows_ref[:, pl.ds(pl.multiple_of((i0 + i1 * h) * 128, 128), 128)]
            right = rows_ref[:, pl.ds(pl.multiple_of((j0 + j1 * h) * 128, 128), 128)]
            part[h, 128 * b:128 * b + 128, :] = dot_hi(left, right, ((0,), (0,)))

    def remote(src, dst, send, recv, dev):
        return pltpu.make_async_remote_copy(src_ref=src, dst_ref=dst, send_sem=send, recv_sem=recv, device_id=dev, device_id_type=MESH)

    fill(other)
    pl.semaphore_wait(barrier, len(peers))
    swap = remote(part.at[other], mate, cs, cr, partner)
    swap.start()
    fill(core)
    swap.wait_recv()
    mine[...] = part[core] + mate[...]
    order = sorted(range(len(plane)), key=lambda j: -(min((j + 1) // yn, xn - (j + 1) // yn) + min((j + 1) % yn, yn - (j + 1) % yn)))
    scatter = []
    for j in order:
        dev, theirs, _ = plane[j]
        c = remote(mine.at[pl.ds(pl.multiple_of(theirs * piece, 8), piece)], inbox.at[j], ps.at[j], pr.at[j], dev)
        c.start()
        scatter.append(c)
    total = mine[pl.ds(pl.multiple_of(own * piece, 8), piece), :]
    for j, c in zip(reversed(order), reversed(scatter)):
        c.wait_recv()
        total = total + inbox[j]
    tower[z] = total
    climb = []
    for j in sorted(range(zn - 1), key=lambda j: -min(j + 1, zn - j - 1)):
        c = remote(tower.at[z], tower.at[z], zs.at[j], zr.at[j], column[j])
        c.start()
        climb.append(c)
    for c in climb:
        c.wait_recv()
    total = tower[0]
    for k in range(1, zn):
        total = total + tower[k]
    full[core, own] = total
    spread = {}
    for j in order:
        dev, _, _ = plane[j]
        spread[j] = remote(full.at[core, own], full.at[core, own], gs.at[j], gr.at[j], dev)
        spread[j].start()
    hand = [remote(full.at[core, own], full.at[core, own], fs.at[len(plane)], fr.at[len(plane)], partner)]
    hand[0].start()
    for j in reversed(order):
        spread[j].wait_recv()
        source = plane[j][2]
        c = remote(full.at[core, source], full.at[core, source], fs.at[j], fr.at[j], partner)
        c.start()
        hand.append(c)
    for c in hand:
        c.wait_recv()
    out_ref[...] = full[...]
    for c in [swap] + scatter + climb + list(spread.values()) + hand:
        c.wait_send()

def gram_sum(rows, dims):
    zn, xn, yn = dims
    n = rows.shape[1]
    pieces = xn * yn
    tall = 5 * 128
    sem = pltpu.SemaphoreType.DMA
    return pl.pallas_call(
        functools.partial(gram_kernel, dims),
        out_shape=jax.ShapeDtypeStruct((2, pieces, tall // pieces, 128), jnp.float32),
        in_specs=[pl.BlockSpec(memory_space=pltpu.VMEM)],
        out_specs=pl.BlockSpec(memory_space=pltpu.VMEM),
        scratch_shapes=[pltpu.VMEM((2, tall, 128), jnp.float32), pltpu.VMEM((tall, 128), jnp.float32), pltpu.VMEM((tall, 128), jnp.float32),
                        pltpu.VMEM((pieces - 1, tall // pieces, 128), jnp.float32), pltpu.VMEM((zn, tall // pieces, 128), jnp.float32),
                        pltpu.VMEM((2, pieces, tall // pieces, 128), jnp.float32),
                        sem, sem, sem((pieces - 1,)), sem((pieces - 1,)), sem((zn - 1,)), sem((zn - 1,)),
                        sem((pieces - 1,)), sem((pieces - 1,)), sem((pieces,)), sem((pieces,))],
        compiler_params=pltpu.CompilerParams(collective_id=0, has_side_effects=True),
        name="gram_sum",
    )(rows)

BLOCKS = tuple(tuple((i0 + i1 * h, j0 + j1 * h) for i0, i1, j0, j1 in HALF) for h in range(2))


def factor_block(a_ref, w_ref, u_ref):
    n = 128
    nv = n // 8
    lane = lax.broadcasted_iota(jnp.int32, (8, n), 1)
    sub = lax.broadcasted_iota(jnp.int32, (8, n), 0)
    a = [a_ref[8 * v:8 * v + 8, :] for v in range(nv)]
    b = [jnp.where(lane == sub + 8 * v, 1.0, 0.0).astype(jnp.float32) for v in range(nv)]
    for r in range(nv):
        col = {}
        for v in range(r, nv):
            for k in range(8):
                col[k, v] = jnp.broadcast_to(a[v][:, 8 * r + k:8 * r + k + 1], (8, n))
        e = {}
        for k in range(8):
            for j in range(k, 8):
                e[k, j] = jnp.broadcast_to(col[j, r][k:k + 1, :], (8, n))
        ra = [jnp.broadcast_to(a[r][k:k + 1, :], (8, n)) for k in range(8)]
        rb = [jnp.broadcast_to(b[r][k:k + 1, :], (8, n)) for k in range(8)]
        for k in range(8):
            rs = lax.rsqrt(e[k, k])
            for j in range(k + 1, 8):
                e[k, j] = e[k, j] * rs
            for i in range(k + 1, 8):
                for j in range(i, 8):
                    e[i, j] = e[i, j] - e[k, i] * e[k, j]
            ra[k] = ra[k] * rs
            rb[k] = rb[k] * rs
            for j in range(k + 1, 8):
                ra[j] = ra[j] - e[k, j] * ra[k]
                rb[j] = rb[j] - e[k, j] * rb[k]
            for v in range(r + 1, nv):
                col[k, v] = col[k, v] * rs
                for j in range(k + 1, 8):
                    col[j, v] = col[j, v] - e[k, j] * col[k, v]
                a[v] = a[v] - col[k, v] * ra[k]
                b[v] = b[v] - col[k, v] * rb[k]
        ua, ub = ra[0], rb[0]
        for k in range(1, 8):
            ua = jnp.where(sub == k, ra[k], ua)
            ub = jnp.where(sub == k, rb[k], ub)
        u_ref[8 * r:8 * r + 8, :] = jnp.where(lane >= sub + 8 * r, ua, 0.0)
        w_ref[8 * r:8 * r + 8, :] = ub

def chol_kernel(scale, g_ref, s_ref, x_ref, t_ref, gw, xs, d_ref, w_ref, u_ref):
    n = gw.shape[0]
    nb = n // 128
    for h in range(2):
        for b, (i, j) in enumerate(BLOCKS[h]):
            gw[128 * i:128 * i + 128, 128 * j:128 * j + 128] = g_ref[h, b]
    xs[...] = s_ref[...] * scale
    t_ref[...] = jnp.zeros_like(t_ref)
    for k in range(nb):
        lo = 128 * k
        hi = lo + 128
        d_ref[...] = gw[lo:hi, lo:hi]
        factor_block(d_ref, w_ref, u_ref)
        w = w_ref[...]
        t_ref[lo:hi, lo:hi] = u_ref[...] * (1.0 / scale)
        if hi < n:
            up = dot_hi(w, gw[lo:hi, hi:n], ((1,), (0,)))
            t_ref[lo:hi, hi:n] = up * (1.0 / scale)
            for i in range(hi, n, 128):
                gw[i:i + 128, i:n] = gw[i:i + 128, i:n] - dot_hi(up[:, i - hi:i - hi + 128], up[:, i - hi:], ((0,), (0,)))
        xk = dot_hi(xs[:, lo:hi], w, ((1,), (1,)))
        x_ref[:, lo:hi] = xk
        if hi < n:
            xs[:, hi:n] = xs[:, hi:n] - dot_hi(xk, up, ((1,), (0,)))


def chol_solve(gram, rows, scale):
    m, n = rows.shape
    return pl.pallas_call(
        functools.partial(chol_kernel, scale),
        out_shape=(jax.ShapeDtypeStruct((m, n), jnp.float32), jax.ShapeDtypeStruct((n, n), jnp.float32)),
        in_specs=[pl.BlockSpec(memory_space=pltpu.VMEM)] * 2,
        out_specs=(pl.BlockSpec(memory_space=pltpu.VMEM),) * 2,
        scratch_shapes=[pltpu.VMEM((n, n), jnp.float32), pltpu.VMEM((m, n), jnp.float32),
                        pltpu.VMEM((128, 128), jnp.float32), pltpu.VMEM((128, 128), jnp.float32),
                        pltpu.VMEM((128, 128), jnp.float32)],
        name="factor_solve",
    )(gram, rows)


def shifted(block, distance):
    count = lax.axis_size("col")
    return lax.ppermute(block, "col", [(i, (i + distance) % count) for i in range(count)])


def body(tile_values, tile_places, tile_counts, sketch):
    tile_stack = tile_values[0, 0]
    tile_size = tile_stack.shape[1]
    sketch_width = sketch.shape[1]
    row_devices = lax.axis_size("row")
    col_devices = lax.axis_size("col")
    local_rows = sketch.shape[0] // row_devices
    chunk_rows = local_rows // tile_size
    half = chunk_rows // 2
    panels = sketch.reshape(-1, tile_size, sketch_width)
    me = lax.axis_index("col")
    plan, span0, span1 = make_plan(tile_places[0, 0], tile_counts[0, 0], me, col_devices, chunk_rows)
    up, down = sparse_sum(plan, span0, tile_stack, panels, 0, (2, half))
    later = sparse_sum(plan, span1, tile_stack, panels, chunk_rows, (2 * (col_devices - 1), half))
    for turn in range(col_devices - 1):
        up = shifted(up, 1) + later[2 * turn]
        down = shifted(down, -1) + later[2 * turn + 1]
    own_rows = jnp.concatenate([up, down], axis=0).reshape(local_rows, sketch_width)
    gram_blocks = gram_sum(own_rows, (row_devices // 8, 4, col_devices)).reshape(2, 5, 128, 128)
    order_scale = math.sqrt(local_rows * row_devices * col_devices)
    basis_rows, upper = chol_solve(gram_blocks, own_rows, order_scale)
    return basis_rows, upper


def solution(mesh):
    in_specs = (
        P("row", "col", None, None, None),
        P("row", "col", None, None),
        P("row", "col"),
        P("col", None),
    )
    out_specs = (P(("row", "col"), None), P())
    return jax.shard_map(body, mesh=mesh, in_specs=in_specs, out_specs=out_specs, check_vma=False)
```

```python
import functools, math
import jax
import jax.numpy as jnp
from jax import lax
from jax.experimental import pallas as pl
from jax.experimental.pallas import tpu as pltpu
from jax.sharding import PartitionSpec as P

GROUP = 4
TURN = 3
RING = 12

def sparse_kernel(base, plan_ref, span_ref, tiles, panels, *rest):
    nout = len(rest) - 6
    outs = rest[:nout]
    lhs, rhs, sums, tsem, psem, osem = rest[nout:]
    first = span_ref[0]
    last = span_ref[1]
    size = tiles.shape[1]
    rows_each = outs[0].shape[0]
    spare = nout * rows_each

    def parts(g, k):
        word = plan_ref[g * GROUP + k]
        s = lax.rem(g, RING)
        live = word >= (1 << 23)
        tile = pltpu.make_async_copy(tiles.at[word & 511], lhs.at[s, :, pl.ds(k * size, size)], tsem.at[s, k])
        panel = pltpu.make_async_copy(panels.at[(word >> 9) & 511], rhs.at[s, pl.ds(k * size, size), :], psem.at[s, k])
        return live, tile, panel, s

    def issue(g):
        for k in range(GROUP):
            live, tile, panel, s = parts(g, k)
            @pl.when(live)
            def _():
                tile.start()
                panel.start()
            if k:
                @pl.when(jnp.logical_not(live))
                def _():
                    lhs[s, :, k * size:(k + 1) * size] = jnp.zeros((size, size), lhs.dtype)
                    rhs[s, k * size:(k + 1) * size, :] = jnp.zeros((size, rhs.shape[2]), rhs.dtype)

    def prime(g, c):
        issue(g)
        return c

    lax.fori_loop(first, jnp.minimum(first + RING - TURN, last), prime, 0)

    def clear(i, c):
        sums[i] = jnp.zeros(sums.shape[1:], sums.dtype)
        return c

    lax.fori_loop(0, sums.shape[0], clear, 0)

    def step(turn, carry):
        g0 = first + turn * TURN
        for u in range(TURN):
            g = g0 + u
            @pl.when(g + RING - TURN < last)
            def _():
                issue(g + RING - TURN)
            @pl.when(g < last)
            def _():
                for k in range(GROUP):
                    live, tile, panel, s = parts(g, k)
                    @pl.when(live)
                    def _():
                        tile.wait()
                        panel.wait()
        for u in range(TURN):
            g = g0 + u
            s = lax.rem(g, RING)
            place = jnp.where(g < last, ((plan_ref[jnp.minimum(g, last - 1) * GROUP] >> 18) & 31) - base, spare)
            prod = jnp.dot(lhs[s], rhs[s], preferred_element_type=jnp.float32)
            sums[place] = sums[place] + prod
        return carry

    lax.fori_loop(0, lax.div(last - first + TURN - 1, TURN), step, 0)
    copies = [pltpu.make_async_copy(sums.at[pl.ds(i * rows_each, rows_each)], o, osem.at[i]) for i, o in enumerate(outs)]
    for c in copies:
        c.start()
    for c in copies:
        c.wait()

def sparse_sum(plan, span, tiles, panels, base, shape):
    nout, rows = shape
    width = panels.shape[2]
    size = tiles.shape[1]
    return pl.pallas_call(
        functools.partial(sparse_kernel, base),
        grid_spec=pltpu.PrefetchScalarGridSpec(
            num_scalar_prefetch=2, grid=(),
            in_specs=[pl.BlockSpec(memory_space=pl.ANY)] * 2,
            out_specs=[pl.BlockSpec(memory_space=pl.ANY)] * nout,
            scratch_shapes=[pltpu.VMEM((RING, size, GROUP * size), tiles.dtype), pltpu.VMEM((RING, GROUP * size, width), panels.dtype),
                            pltpu.VMEM((nout * rows + 1, size, width), jnp.float32),
                            pltpu.SemaphoreType.DMA((RING, GROUP)), pltpu.SemaphoreType.DMA((RING, GROUP)), pltpu.SemaphoreType.DMA((nout,))]),
        out_shape=[jax.ShapeDtypeStruct((rows, size, width), jnp.float32)] * nout,
        compiler_params=pltpu.CompilerParams(vmem_limit_bytes=60 << 20),
        cost_estimate=pl.CostEstimate(flops=2 * 360 * 128 * 128 * 512 * rows * nout // 24, bytes_accessed=50_000_000 * rows * nout // 24, transcendentals=0),
        name="tile_sums",
    )(plan, span, tiles, panels)

def make_plan(places, count, me, ncol, chunk_rows):
    rows = places[0]
    cols = places[1]
    n = rows.shape[0]
    nplace = ncol * chunk_rows
    ids = jnp.arange(n, dtype=jnp.int32)
    half = chunk_rows // 2
    dest = rows // chunk_rows
    sub = rows % chunk_rows
    step = jnp.where(sub < half, (me - 1 - dest) % ncol, (dest - 1 - me) % ncol)
    live = ids < count
    place = jnp.where(live, step * chunk_rows + sub, nplace)
    rank = jnp.sum(((place[None, :] == place[:, None]) & (ids[None, :] < ids[:, None])).astype(jnp.int32), axis=1)
    which = jnp.arange(nplace, dtype=jnp.int32)
    held = jnp.sum((place[None, :] == which[:, None]).astype(jnp.int32), axis=1)
    groups = (held + GROUP - 1) // GROUP
    ahead = jnp.sum(jnp.where(which[None, :] < place[:, None], groups[None, :], 0), axis=1)
    spot = jnp.where(live, ahead * GROUP + rank, -1)
    word = ids | (cols << 9) | (place << 18) | (1 << 23)
    total = -(-(n // GROUP + nplace) * GROUP // 128) * 128
    plan = jnp.sum(jnp.where(spot[None, :] == jnp.arange(total, dtype=jnp.int32)[:, None], word[None, :], 0), axis=1)
    n0 = jnp.sum(jnp.where(which < chunk_rows, groups, 0))
    n1 = jnp.sum(groups)
    return plan, jnp.stack([jnp.int32(0), n0]), jnp.stack([n0, n1])


HI = lax.Precision.HIGHEST

def dot_hi(a, b, dims):
    return lax.dot_general(a, b, (dims, ((), ())), precision=HI, preferred_element_type=jnp.float32)

MESH = pl.DeviceIdType.MESH
BLOCKS = (((0, 0), (2, 2), (0, 1), (2, 3), (0, 2)), ((1, 1), (3, 3), (1, 2), (0, 3), (1, 3)))
SPOT = {ij: (h, b) for h in range(2) for b, ij in enumerate(BLOCKS[h])}

def ring_kernel(dims, up_ref, down_ref, later_ref, rows_ref, out_ref,
                head, later, box1, box2, part, mate, mine, inbox, tower, full,
                hsem, lsem, s1, r1, s2, r2, cs, cr, ps, pr, zs, zr, gs, gr, fs, fr):
    zn, xn, yn = dims
    row = lax.axis_index("row")
    y = lax.axis_index("col")
    core = lax.rem(row, 2)
    x = lax.rem(row // 2, xn)
    z = row // (2 * xn)
    other = 1 - core
    count = up_ref.shape[0]
    tall = up_ref.shape[1]

    def at(zz, xx, yy, cc):
        return ((zz * xn + xx) * 2 + cc, yy)

    partner = at(z, x, y, other)
    plane = []
    for j in range(1, xn * yn):
        dx, dy = j // yn, j % yn
        plane.append((at(z, lax.rem(x + dx, xn), lax.rem(y + dy, yn), core),
                      lax.rem(x + dx, xn) * yn + lax.rem(y + dy, yn),
                      lax.rem(x + xn - dx, xn) * yn + lax.rem(y + yn - dy, yn)))
    column = [at(lax.rem(z + j, zn), x, y, core) for j in range(1, zn)]
    own = x * yn + y
    piece = mine.shape[0] // (xn * yn)
    ring = [(row, lax.rem(y + 1, yn)), (row, lax.rem(y + yn - 1, yn))]

    barrier = pltpu.get_barrier_semaphore()
    peers = [partner] + [p[0] for p in plane] + column
    for peer in peers:
        pl.semaphore_signal(barrier, inc=1, device_id=peer, device_id_type=MESH)

    def remote(src, dst, send, recv, dev):
        return pltpu.make_async_remote_copy(src_ref=src, dst_ref=dst, send_sem=send, recv_sem=recv, device_id=dev, device_id_type=MESH)

    def head_copy(i, d):
        return pltpu.make_async_copy((up_ref, down_ref)[d].at[i], head.at[d, i], hsem.at[d, i])

    def later_copy(step, i, d):
        p = (2 * step + d) * count + i
        return pltpu.make_async_copy(later_ref.at[p], later.at[step, d, i], lsem.at[step, d, i])

    def hop1(i, d):
        return remote(head.at[d, i], box1.at[d, i], s1.at[d, i], r1.at[d, i], ring[d])

    def hop2(i, d):
        return remote(box1.at[d, i], box2.at[d, i], s2.at[d, i], r2.at[d, i], ring[d])

    for i in range(count):
        for d in range(2):
            head_copy(i, d).start()
            later_copy(0, i, d).start()
    for step in range(1, 3):
        for i in range(count):
            for d in range(2):
                later_copy(step, i, d).start()
    part[...] = jnp.zeros_like(part)
    pl.semaphore_wait(barrier, len(peers))

    def first(i, c):
        for d in range(2):
            head_copy(i, d).wait()
            later_copy(0, i, d).wait()
            head[d, i] = head[d, i] + later[0, d, i]
            hop1(i, d).start()
        return c

    lax.fori_loop(0, count, first, 0)

    def second(i, c):
        for d in range(2):
            later_copy(1, i, d).wait()
            hop1(i, d).wait_recv()
            box1[d, i] = box1[d, i] + later[1, d, i]
            hop2(i, d).start()
        return c

    lax.fori_loop(0, count, second, 0)

    def third(i, c):
        for d in range(2):
            later_copy(2, i, d).wait()
            hop2(i, d).wait_recv()
            total = box2[d, i] + later[2, d, i]
            rows_ref[d, i] = total
            for a in range(4):
                got = dot_hi(total[:, 128 * a:128 * a + 128], total[:, 128 * a:], ((0,), (0,)))
                for j in range(a, 4):
                    h, b = SPOT[a, j]
                    part[h, 128 * b:128 * b + 128, :] = part[h, 128 * b:128 * b + 128, :] + got[:, 128 * (j - a):128 * (j - a) + 128]
        return c

    lax.fori_loop(0, count, third, 0)

    swap = remote(part.at[other], mate, cs, cr, partner)
    swap.start()
    swap.wait_recv()
    mine[...] = part[core] + mate[...]
    order = sorted(range(len(plane)), key=lambda j: -(min((j + 1) // yn, xn - (j + 1) // yn) + min((j + 1) % yn, yn - (j + 1) % yn)))
    scatter = []
    for j in order:
        dev, theirs, _ = plane[j]
        c = remote(mine.at[pl.ds(pl.multiple_of(theirs * piece, 8), piece)], inbox.at[j], ps.at[j], pr.at[j], dev)
        c.start()
        scatter.append(c)
    total = mine[pl.ds(pl.multiple_of(own * piece, 8), piece), :]
    for j, c in zip(reversed(order), reversed(scatter)):
        c.wait_recv()
        total = total + inbox[j]
    tower[z] = total
    climb = []
    for j in sorted(range(zn - 1), key=lambda j: -min(j + 1, zn - j - 1)):
        c = remote(tower.at[z], tower.at[z], zs.at[j], zr.at[j], column[j])
        c.start()
        climb.append(c)
    for c in climb:
        c.wait_recv()
    total = tower[0]
    for k in range(1, zn):
        total = total + tower[k]
    full[core, own] = total
    spread = {}
    for j in order:
        dev, _, _ = plane[j]
        spread[j] = remote(full.at[core, own], full.at[core, own], gs.at[j], gr.at[j], dev)
        spread[j].start()
    hand = [remote(full.at[core, own], full.at[core, own], fs.at[len(plane)], fr.at[len(plane)], partner)]
    hand[0].start()
    for j in reversed(order):
        spread[j].wait_recv()
        source = plane[j][2]
        c = remote(full.at[core, source], full.at[core, source], fs.at[j], fr.at[j], partner)
        c.start()
        hand.append(c)
    for c in hand:
        c.wait_recv()
    out_ref[...] = full[...]
    for c in [swap] + scatter + climb + list(spread.values()) + hand:
        c.wait_send()

    def drain(i, c):
        for d in range(2):
            hop1(i, d).wait_send()
            hop2(i, d).wait_send()
        return c

    lax.fori_loop(0, count, drain, 0)

def ring_sum(up, down, later, dims):
    zn, xn, yn = dims
    count, tall, n = up.shape
    pieces = xn * yn
    deep = 5 * 128
    sem = pltpu.SemaphoreType.DMA
    f32 = jnp.float32
    return pl.pallas_call(
        functools.partial(ring_kernel, dims),
        out_shape=(jax.ShapeDtypeStruct((2, count, tall, n), f32), jax.ShapeDtypeStruct((2, pieces, deep // pieces, 128), f32)),
        in_specs=[pl.BlockSpec(memory_space=pl.ANY)] * 3,
        out_specs=(pl.BlockSpec(memory_space=pltpu.VMEM),) * 2,
        scratch_shapes=[pltpu.VMEM((2, count, tall, n), f32), pltpu.VMEM((3, 2, count, tall, n), f32),
                        pltpu.VMEM((2, count, tall, n), f32), pltpu.VMEM((2, count, tall, n), f32),
                        pltpu.VMEM((2, deep, 128), f32), pltpu.VMEM((deep, 128), f32), pltpu.VMEM((deep, 128), f32),
                        pltpu.VMEM((pieces - 1, deep // pieces, 128), f32), pltpu.VMEM((zn, deep // pieces, 128), f32),
                        pltpu.VMEM((2, pieces, deep // pieces, 128), f32),
                        sem((2, count)), sem((3, 2, count)), sem((2, count)), sem((2, count)), sem((2, count)), sem((2, count)),
                        sem, sem, sem((pieces - 1,)), sem((pieces - 1,)), sem((zn - 1,)), sem((zn - 1,)),
                        sem((pieces - 1,)), sem((pieces - 1,)), sem((pieces,)), sem((pieces,))],
        compiler_params=pltpu.CompilerParams(collective_id=0, has_side_effects=True, vmem_limit_bytes=60 << 20),
        name="ring_sum",
    )(up, down, later)


def factor_block(a_ref, w_ref, u_ref):
    n = 128
    nv = n // 8
    lane = lax.broadcasted_iota(jnp.int32, (8, n), 1)
    sub = lax.broadcasted_iota(jnp.int32, (8, n), 0)
    a = [a_ref[8 * v:8 * v + 8, :] for v in range(nv)]
    b = [jnp.where(lane == sub + 8 * v, 1.0, 0.0).astype(jnp.float32) for v in range(nv)]
    for r in range(nv):
        col = {}
        for v in range(r, nv):
            for k in range(8):
                col[k, v] = jnp.broadcast_to(a[v][:, 8 * r + k:8 * r + k + 1], (8, n))
        e = {}
        for k in range(8):
            for j in range(k, 8):
                e[k, j] = jnp.broadcast_to(col[j, r][k:k + 1, :], (8, n))
        ra = [jnp.broadcast_to(a[r][k:k + 1, :], (8, n)) for k in range(8)]
        rb = [jnp.broadcast_to(b[r][k:k + 1, :], (8, n)) for k in range(8)]
        for k in range(8):
            rs = lax.rsqrt(e[k, k])
            for j in range(k + 1, 8):
                e[k, j] = e[k, j] * rs
            for i in range(k + 1, 8):
                for j in range(i, 8):
                    e[i, j] = e[i, j] - e[k, i] * e[k, j]
            ra[k] = ra[k] * rs
            rb[k] = rb[k] * rs
            for j in range(k + 1, 8):
                ra[j] = ra[j] - e[k, j] * ra[k]
                rb[j] = rb[j] - e[k, j] * rb[k]
            for v in range(r + 1, nv):
                col[k, v] = col[k, v] * rs
                for j in range(k + 1, 8):
                    col[j, v] = col[j, v] - e[k, j] * col[k, v]
                a[v] = a[v] - col[k, v] * ra[k]
                b[v] = b[v] - col[k, v] * rb[k]
        ua, ub = ra[0], rb[0]
        for k in range(1, 8):
            ua = jnp.where(sub == k, ra[k], ua)
            ub = jnp.where(sub == k, rb[k], ub)
        u_ref[8 * r:8 * r + 8, :] = jnp.where(lane >= sub + 8 * r, ua, 0.0)
        w_ref[8 * r:8 * r + 8, :] = ub

def chol_kernel(scale, g_ref, s_ref, x_ref, t_ref, gw, xs, d_ref, w_ref, u_ref):
    n = gw.shape[0]
    nb = n // 128
    for h in range(2):
        for b, (i, j) in enumerate(BLOCKS[h]):
            gw[128 * i:128 * i + 128, 128 * j:128 * j + 128] = g_ref[h, b]
    xs[...] = s_ref[...] * scale
    t_ref[...] = jnp.zeros_like(t_ref)
    for k in range(nb):
        lo = 128 * k
        hi = lo + 128
        d_ref[...] = gw[lo:hi, lo:hi]
        factor_block(d_ref, w_ref, u_ref)
        w = w_ref[...]
        t_ref[lo:hi, lo:hi] = u_ref[...] * (1.0 / scale)
        if hi < n:
            up = dot_hi(w, gw[lo:hi, hi:n], ((1,), (0,)))
            t_ref[lo:hi, hi:n] = up * (1.0 / scale)
            for i in range(hi, n, 128):
                gw[i:i + 128, i:n] = gw[i:i + 128, i:n] - dot_hi(up[:, i - hi:i - hi + 128], up[:, i - hi:], ((0,), (0,)))
        xk = dot_hi(xs[:, lo:hi], w, ((1,), (1,)))
        x_ref[:, lo:hi] = xk
        if hi < n:
            xs[:, hi:n] = xs[:, hi:n] - dot_hi(xk, up, ((1,), (0,)))


def chol_solve(gram, rows, scale):
    m, n = rows.shape
    return pl.pallas_call(
        functools.partial(chol_kernel, scale),
        out_shape=(jax.ShapeDtypeStruct((m, n), jnp.float32), jax.ShapeDtypeStruct((n, n), jnp.float32)),
        in_specs=[pl.BlockSpec(memory_space=pltpu.VMEM)] * 2,
        out_specs=(pl.BlockSpec(memory_space=pltpu.VMEM),) * 2,
        scratch_shapes=[pltpu.VMEM((n, n), jnp.float32), pltpu.VMEM((m, n), jnp.float32),
                        pltpu.VMEM((128, 128), jnp.float32), pltpu.VMEM((128, 128), jnp.float32),
                        pltpu.VMEM((128, 128), jnp.float32)],
        name="factor_solve",
    )(gram, rows)


def shifted(block, distance):
    count = lax.axis_size("col")
    return lax.ppermute(block, "col", [(i, (i + distance) % count) for i in range(count)])


def body(tile_values, tile_places, tile_counts, sketch):
    tile_stack = tile_values[0, 0]
    tile_size = tile_stack.shape[1]
    sketch_width = sketch.shape[1]
    row_devices = lax.axis_size("row")
    col_devices = lax.axis_size("col")
    local_rows = sketch.shape[0] // row_devices
    chunk_rows = local_rows // tile_size
    half = chunk_rows // 2
    panels = sketch.reshape(-1, tile_size, sketch_width)
    me = lax.axis_index("col")
    plan, span0, span1 = make_plan(tile_places[0, 0], tile_counts[0, 0], me, col_devices, chunk_rows)
    up, down = sparse_sum(plan, span0, tile_stack, panels, 0, (2, half))
    (later,) = sparse_sum(plan, span1, tile_stack, panels, chunk_rows, (1, chunk_rows * (col_devices - 1)))
    own, gram = ring_sum(shifted(up, 1), shifted(down, -1), later, (row_devices // 8, 4, col_devices))
    own_rows = own.reshape(local_rows, sketch_width)
    gram_blocks = gram.reshape(2, 5, 128, 128)
    order_scale = math.sqrt(local_rows * row_devices * col_devices)
    basis_rows, upper = chol_solve(gram_blocks, own_rows, order_scale)
    return basis_rows, upper


def solution(mesh):
    in_specs = (
        P("row", "col", None, None, None),
        P("row", "col", None, None),
        P("row", "col"),
        P("col", None),
    )
    out_specs = (P(("row", "col"), None), P())
    return jax.shard_map(body, mesh=mesh, in_specs=in_specs, out_specs=out_specs, check_vma=False)
```

```python
import functools, math
import jax
import jax.numpy as jnp
from jax import lax
from jax.experimental import pallas as pl
from jax.experimental.pallas import tpu as pltpu
from jax.sharding import PartitionSpec as P

GROUP = 4
TURN = 3
RING = 12
SPANS = 7 * 128

def sparse_kernel(base, stage, plan_ref, tiles, panels, *rest):
    nout = len(rest) - 6
    outs = rest[:nout]
    lhs, rhs, sums, tsem, psem, osem = rest[nout:]
    first = plan_ref[SPANS + stage]
    last = plan_ref[SPANS + stage + 1]
    size = tiles.shape[1]
    rows_each = outs[0].shape[0]
    spare = nout * rows_each

    def parts(g, k):
        word = plan_ref[g * GROUP + k]
        s = lax.rem(g, RING)
        live = word >= (1 << 23)
        tile = pltpu.make_async_copy(tiles.at[word & 511], lhs.at[s, :, pl.ds(k * size, size)], tsem.at[s, k])
        panel = pltpu.make_async_copy(panels.at[(word >> 9) & 511], rhs.at[s, pl.ds(k * size, size), :], psem.at[s, k])
        return live, tile, panel, s

    def issue(g):
        for k in range(GROUP):
            live, tile, panel, s = parts(g, k)
            @pl.when(live)
            def _():
                tile.start()
                panel.start()
            if k:
                @pl.when(jnp.logical_not(live))
                def _():
                    lhs[s, :, k * size:(k + 1) * size] = jnp.zeros((size, size), lhs.dtype)
                    rhs[s, k * size:(k + 1) * size, :] = jnp.zeros((size, rhs.shape[2]), rhs.dtype)

    def prime(g, c):
        issue(g)
        return c

    lax.fori_loop(first, jnp.minimum(first + RING - TURN, last), prime, 0)

    def clear(i, c):
        sums[i] = jnp.zeros(sums.shape[1:], sums.dtype)
        return c

    lax.fori_loop(0, sums.shape[0], clear, 0)

    def step(turn, carry):
        g0 = first + turn * TURN
        for u in range(TURN):
            g = g0 + u
            @pl.when(g + RING - TURN < last)
            def _():
                issue(g + RING - TURN)
            @pl.when(g < last)
            def _():
                for k in range(GROUP):
                    live, tile, panel, s = parts(g, k)
                    @pl.when(live)
                    def _():
                        tile.wait()
                        panel.wait()
        for u in range(TURN):
            g = g0 + u
            s = lax.rem(g, RING)
            place = jnp.where(g < last, ((plan_ref[jnp.minimum(g, last - 1) * GROUP] >> 18) & 31) - base, spare)
            prod = jnp.dot(lhs[s], rhs[s], preferred_element_type=jnp.float32)
            sums[place] = sums[place] + prod
        return carry

    lax.fori_loop(0, lax.div(last - first + TURN - 1, TURN), step, 0)
    copies = [pltpu.make_async_copy(sums.at[pl.ds(i * rows_each, rows_each)], o, osem.at[i]) for i, o in enumerate(outs)]
    for c in copies:
        c.start()
    for c in copies:
        c.wait()

def sparse_sum(plan, stage, tiles, panels, base, shape):
    nout, rows = shape
    width = panels.shape[2]
    size = tiles.shape[1]
    return pl.pallas_call(
        functools.partial(sparse_kernel, base, stage),
        grid_spec=pltpu.PrefetchScalarGridSpec(
            num_scalar_prefetch=1, grid=(),
            in_specs=[pl.BlockSpec(memory_space=pl.ANY)] * 2,
            out_specs=[pl.BlockSpec(memory_space=pl.ANY)] * nout,
            scratch_shapes=[pltpu.VMEM((RING, size, GROUP * size), tiles.dtype), pltpu.VMEM((RING, GROUP * size, width), panels.dtype),
                            pltpu.VMEM((nout * rows + 1, size, width), jnp.float32),
                            pltpu.SemaphoreType.DMA((RING, GROUP)), pltpu.SemaphoreType.DMA((RING, GROUP)), pltpu.SemaphoreType.DMA((nout,))]),
        out_shape=[jax.ShapeDtypeStruct((rows, size, width), jnp.float32)] * nout,
        compiler_params=pltpu.CompilerParams(vmem_limit_bytes=67_000_000),
        cost_estimate=pl.CostEstimate(flops=2 * 360 * 128 * 128 * 512 * rows * nout // 24, bytes_accessed=50_000_000 * rows * nout // 24, transcendentals=0),
        name="tile_sums",
    )(plan, tiles, panels)

HI = lax.Precision.HIGHEST

def dot_hi(a, b, dims):
    return lax.dot_general(a, b, (dims, ((), ())), precision=HI, preferred_element_type=jnp.float32)

def plan_kernel(ncol, chunk, count_ref, places_ref, plan_ref, wide):
    me = lax.axis_index("col")
    width = wide.shape[1]
    wide[...] = jnp.zeros_like(wide)
    wide[:, :places_ref.shape[1]] = places_ref[...]
    rows = wide[0:1, :]
    cols = wide[1:2, :]
    ids = lax.broadcasted_iota(jnp.int32, (1, width), 1)
    live = ids < count_ref[0, 0]
    dest = jnp.zeros_like(rows)
    for q in range(1, ncol):
        dest = dest + (rows >= q * chunk).astype(jnp.int32)
    sub = rows - dest * chunk
    step = jnp.where(sub < chunk // 2, (me + 2 * ncol - 1 - dest) & (ncol - 1), (dest + 2 * ncol - 1 - me) & (ncol - 1))
    place = step * chunk + sub
    shelf = lax.broadcasted_iota(jnp.int32, (32, width), 0)
    held = jnp.where(shelf == jnp.where(live, place, 99), 1.0, 0.0)
    before = lax.broadcasted_iota(jnp.int32, (width, width), 0) < lax.broadcasted_iota(jnp.int32, (width, width), 1)
    rank = jnp.dot(held.astype(jnp.bfloat16), jnp.where(before, 1.0, 0.0).astype(jnp.bfloat16), preferred_element_type=jnp.float32)
    groups = (jnp.sum(held, axis=1, keepdims=True).astype(jnp.int32) + GROUP - 1) // GROUP
    wide_groups = jnp.broadcast_to(groups.astype(jnp.float32), (32, 128))
    under = lax.broadcasted_iota(jnp.int32, (32, 32), 1) < lax.broadcasted_iota(jnp.int32, (32, 32), 0)
    ahead = jnp.dot(jnp.where(under, 1.0, 0.0).astype(jnp.bfloat16), wide_groups.astype(jnp.bfloat16), preferred_element_type=jnp.float32)
    spot = jnp.sum(held * (rank + GROUP * ahead[:, 0:1]), axis=0, keepdims=True).astype(jnp.int32)
    spot = jnp.where(live, spot, -1)
    word = (ids + cols * 512 + place * (1 << 18) + (1 << 23)).astype(jnp.float32)
    high = jnp.where(lax.broadcasted_iota(jnp.int32, (8, width), 0) == (spot >> 7), word, 0.0)
    low = jnp.where(lax.broadcasted_iota(jnp.int32, (128, width), 0) == (spot & 127), 1.0, 0.0)
    plan = dot_hi(high, low, ((1,), (1,))).astype(jnp.int32)
    r8 = lax.broadcasted_iota(jnp.int32, (8, 128), 0)
    c8 = lax.broadcasted_iota(jnp.int32, (8, 128), 1)
    shelf8 = lax.broadcasted_iota(jnp.int32, (32, 128), 0)
    n0 = jnp.sum(jnp.where(shelf8 < chunk, wide_groups, 0.0), axis=0, keepdims=True).astype(jnp.int32)
    n1 = jnp.sum(wide_groups, axis=0, keepdims=True).astype(jnp.int32)
    plan_ref[...] = jnp.where(r8 == 7, jnp.where(c8 == 1, n0, jnp.where(c8 == 2, n1, 0)), plan)

def make_plan(places, count, ncol, chunk_rows):
    width = -(-places.shape[1] // 128) * 128
    return pl.pallas_call(
        functools.partial(plan_kernel, ncol, chunk_rows),
        out_shape=jax.ShapeDtypeStruct((8, 128), jnp.int32),
        in_specs=[pl.BlockSpec(memory_space=pltpu.SMEM), pl.BlockSpec(memory_space=pltpu.VMEM)],
        out_specs=pl.BlockSpec(memory_space=pltpu.VMEM),
        scratch_shapes=[pltpu.VMEM((2, width), jnp.int32)],
        name="tile_plan",
    )(count, places).reshape(8 * 128)


MESH = pl.DeviceIdType.MESH
BLOCKS = (((0, 0), (2, 2), (0, 1), (2, 3), (0, 2)), ((1, 1), (3, 3), (1, 2), (0, 3), (1, 3)))
SPOT = {ij: (h, b) for h in range(2) for b, ij in enumerate(BLOCKS[h])}

def ring_kernel(dims, up_ref, down_ref, later_ref, rows_ref, out_ref,
                head, later, box1, box2, part, mate, mine, inbox, tower, full,
                hsem, lsem, s1, r1, s2, r2, cs, cr, ps, pr, zs, zr, gs, gr, fs, fr):
    zn, xn, yn = dims
    row = lax.axis_index("row")
    y = lax.axis_index("col")
    core = lax.rem(row, 2)
    x = lax.rem(row // 2, xn)
    z = row // (2 * xn)
    other = 1 - core
    count = up_ref.shape[0]
    tall = up_ref.shape[1]

    def at(zz, xx, yy, cc):
        return ((zz * xn + xx) * 2 + cc, yy)

    partner = at(z, x, y, other)
    plane = []
    for j in range(1, xn * yn):
        dx, dy = j // yn, j % yn
        plane.append((at(z, lax.rem(x + dx, xn), lax.rem(y + dy, yn), core),
                      lax.rem(x + dx, xn) * yn + lax.rem(y + dy, yn),
                      lax.rem(x + xn - dx, xn) * yn + lax.rem(y + yn - dy, yn)))
    column = [at(lax.rem(z + j, zn), x, y, core) for j in range(1, zn)]
    own = x * yn + y
    piece = mine.shape[0] // (xn * yn)
    ring = [(row, lax.rem(y + 1, yn)), (row, lax.rem(y + yn - 1, yn))]

    barrier = pltpu.get_barrier_semaphore()
    peers = [partner] + [p[0] for p in plane] + column
    for peer in peers:
        pl.semaphore_signal(barrier, inc=1, device_id=peer, device_id_type=MESH)

    def remote(src, dst, send, recv, dev):
        return pltpu.make_async_remote_copy(src_ref=src, dst_ref=dst, send_sem=send, recv_sem=recv, device_id=dev, device_id_type=MESH)

    def head_copy(i, d):
        return pltpu.make_async_copy((up_ref, down_ref)[d].at[i], head.at[d, i], hsem.at[d, i])

    def later_copy(step, i, d):
        p = (2 * step + d) * count + i
        return pltpu.make_async_copy(later_ref.at[p], later.at[step, d, i], lsem.at[step, d, i])

    def hop1(i, d):
        return remote(head.at[d, i], box1.at[d, i], s1.at[d, i], r1.at[d, i], ring[d])

    def hop2(i, d):
        return remote(box1.at[d, i], box2.at[d, i], s2.at[d, i], r2.at[d, i], ring[d])

    for i in range(count):
        for d in range(2):
            head_copy(i, d).start()
            later_copy(0, i, d).start()
    for step in range(1, 3):
        for i in range(count):
            for d in range(2):
                later_copy(step, i, d).start()
    part[...] = jnp.zeros_like(part)
    pl.semaphore_wait(barrier, len(peers))

    def first(i, c):
        for d in range(2):
            head_copy(i, d).wait()
            later_copy(0, i, d).wait()
            head[d, i] = head[d, i] + later[0, d, i]
            hop1(i, d).start()
        return c

    lax.fori_loop(0, count, first, 0)

    def second(i, c):
        for d in range(2):
            later_copy(1, i, d).wait()
            hop1(i, d).wait_recv()
            box1[d, i] = box1[d, i] + later[1, d, i]
            hop2(i, d).start()
        return c

    lax.fori_loop(0, count, second, 0)

    def third(i, c):
        for d in range(2):
            later_copy(2, i, d).wait()
            hop2(i, d).wait_recv()
            total = box2[d, i] + later[2, d, i]
            rows_ref[d, i] = total
            for a in range(4):
                got = dot_hi(total[:, 128 * a:128 * a + 128], total[:, 128 * a:], ((0,), (0,)))
                for j in range(a, 4):
                    h, b = SPOT[a, j]
                    part[h, 128 * b:128 * b + 128, :] = part[h, 128 * b:128 * b + 128, :] + got[:, 128 * (j - a):128 * (j - a) + 128]
        return c

    lax.fori_loop(0, count, third, 0)

    swap = remote(part.at[other], mate, cs, cr, partner)
    swap.start()
    swap.wait_recv()
    mine[...] = part[core] + mate[...]
    order = sorted(range(len(plane)), key=lambda j: -(min((j + 1) // yn, xn - (j + 1) // yn) + min((j + 1) % yn, yn - (j + 1) % yn)))
    scatter = []
    for j in order:
        dev, theirs, _ = plane[j]
        c = remote(mine.at[pl.ds(pl.multiple_of(theirs * piece, 8), piece)], inbox.at[j], ps.at[j], pr.at[j], dev)
        c.start()
        scatter.append(c)
    total = mine[pl.ds(pl.multiple_of(own * piece, 8), piece), :]
    for j, c in zip(reversed(order), reversed(scatter)):
        c.wait_recv()
        total = total + inbox[j]
    tower[z] = total
    climb = []
    for j in sorted(range(zn - 1), key=lambda j: -min(j + 1, zn - j - 1)):
        c = remote(tower.at[z], tower.at[z], zs.at[j], zr.at[j], column[j])
        c.start()
        climb.append(c)
    for c in climb:
        c.wait_recv()
    total = tower[0]
    for k in range(1, zn):
        total = total + tower[k]
    full[core, own] = total
    spread = {}
    for j in order:
        dev, _, _ = plane[j]
        spread[j] = remote(full.at[core, own], full.at[core, own], gs.at[j], gr.at[j], dev)
        spread[j].start()
    hand = [remote(full.at[core, own], full.at[core, own], fs.at[len(plane)], fr.at[len(plane)], partner)]
    hand[0].start()
    for j in reversed(order):
        spread[j].wait_recv()
        source = plane[j][2]
        c = remote(full.at[core, source], full.at[core, source], fs.at[j], fr.at[j], partner)
        c.start()
        hand.append(c)
    for c in hand:
        c.wait_recv()
    out_ref[...] = full[...]
    for c in [swap] + scatter + climb + list(spread.values()) + hand:
        c.wait_send()

    def drain(i, c):
        for d in range(2):
            hop1(i, d).wait_send()
            hop2(i, d).wait_send()
        return c

    lax.fori_loop(0, count, drain, 0)

def ring_sum(up, down, later, dims):
    zn, xn, yn = dims
    count, tall, n = up.shape
    pieces = xn * yn
    deep = 5 * 128
    sem = pltpu.SemaphoreType.DMA
    f32 = jnp.float32
    return pl.pallas_call(
        functools.partial(ring_kernel, dims),
        out_shape=(jax.ShapeDtypeStruct((2, count, tall, n), f32), jax.ShapeDtypeStruct((2, pieces, deep // pieces, 128), f32)),
        in_specs=[pl.BlockSpec(memory_space=pl.ANY)] * 3,
        out_specs=(pl.BlockSpec(memory_space=pltpu.VMEM),) * 2,
        scratch_shapes=[pltpu.VMEM((2, count, tall, n), f32), pltpu.VMEM((3, 2, count, tall, n), f32),
                        pltpu.VMEM((2, count, tall, n), f32), pltpu.VMEM((2, count, tall, n), f32),
                        pltpu.VMEM((2, deep, 128), f32), pltpu.VMEM((deep, 128), f32), pltpu.VMEM((deep, 128), f32),
                        pltpu.VMEM((pieces - 1, deep // pieces, 128), f32), pltpu.VMEM((zn, deep // pieces, 128), f32),
                        pltpu.VMEM((2, pieces, deep // pieces, 128), f32),
                        sem((2, count)), sem((3, 2, count)), sem((2, count)), sem((2, count)), sem((2, count)), sem((2, count)),
                        sem, sem, sem((pieces - 1,)), sem((pieces - 1,)), sem((zn - 1,)), sem((zn - 1,)),
                        sem((pieces - 1,)), sem((pieces - 1,)), sem((pieces,)), sem((pieces,))],
        compiler_params=pltpu.CompilerParams(collective_id=0, has_side_effects=True, vmem_limit_bytes=67_000_000),
        name="ring_sum",
    )(up, down, later)


def factor_block(a_ref, w_ref, u_ref):
    n = 128
    nv = n // 8
    lane = lax.broadcasted_iota(jnp.int32, (8, n), 1)
    sub = lax.broadcasted_iota(jnp.int32, (8, n), 0)
    a = [a_ref[8 * v:8 * v + 8, :] for v in range(nv)]
    b = [jnp.where(lane == sub + 8 * v, 1.0, 0.0).astype(jnp.float32) for v in range(nv)]
    for r in range(nv):
        col = {}
        for v in range(r, nv):
            for k in range(8):
                col[k, v] = jnp.broadcast_to(a[v][:, 8 * r + k:8 * r + k + 1], (8, n))
        e = {}
        for k in range(8):
            for j in range(k, 8):
                e[k, j] = jnp.broadcast_to(col[j, r][k:k + 1, :], (8, n))
        ra = [jnp.broadcast_to(a[r][k:k + 1, :], (8, n)) for k in range(8)]
        rb = [jnp.broadcast_to(b[r][k:k + 1, :], (8, n)) for k in range(8)]
        for k in range(8):
            rs = lax.rsqrt(e[k, k])
            for j in range(k + 1, 8):
                e[k, j] = e[k, j] * rs
            for i in range(k + 1, 8):
                for j in range(i, 8):
                    e[i, j] = e[i, j] - e[k, i] * e[k, j]
            ra[k] = ra[k] * rs
            rb[k] = rb[k] * rs
            for j in range(k + 1, 8):
                ra[j] = ra[j] - e[k, j] * ra[k]
                rb[j] = rb[j] - e[k, j] * rb[k]
            for v in range(r + 1, nv):
                col[k, v] = col[k, v] * rs
                for j in range(k + 1, 8):
                    col[j, v] = col[j, v] - e[k, j] * col[k, v]
                a[v] = a[v] - col[k, v] * ra[k]
                b[v] = b[v] - col[k, v] * rb[k]
        ua, ub = ra[0], rb[0]
        for k in range(1, 8):
            ua = jnp.where(sub == k, ra[k], ua)
            ub = jnp.where(sub == k, rb[k], ub)
        u_ref[8 * r:8 * r + 8, :] = jnp.where(lane >= sub + 8 * r, ua, 0.0)
        w_ref[8 * r:8 * r + 8, :] = ub

def chol_kernel(scale, g_ref, s_ref, x_ref, t_ref, gw, xs, d_ref, w_ref, u_ref):
    n = gw.shape[0]
    nb = n // 128
    for h in range(2):
        for b, (i, j) in enumerate(BLOCKS[h]):
            gw[128 * i:128 * i + 128, 128 * j:128 * j + 128] = g_ref[h, b]
    xs[...] = s_ref[...] * scale
    t_ref[...] = jnp.zeros_like(t_ref)
    for k in range(nb):
        lo = 128 * k
        hi = lo + 128
        d_ref[...] = gw[lo:hi, lo:hi]
        factor_block(d_ref, w_ref, u_ref)
        w = w_ref[...]
        t_ref[lo:hi, lo:hi] = u_ref[...] * (1.0 / scale)
        if hi < n:
            up = dot_hi(w, gw[lo:hi, hi:n], ((1,), (0,)))
            t_ref[lo:hi, hi:n] = up * (1.0 / scale)
            for i in range(hi, n, 128):
                gw[i:i + 128, i:n] = gw[i:i + 128, i:n] - dot_hi(up[:, i - hi:i - hi + 128], up[:, i - hi:], ((0,), (0,)))
        xk = dot_hi(xs[:, lo:hi], w, ((1,), (1,)))
        x_ref[:, lo:hi] = xk
        if hi < n:
            xs[:, hi:n] = xs[:, hi:n] - dot_hi(xk, up, ((1,), (0,)))


def chol_solve(gram, rows, scale):
    m, n = rows.shape
    return pl.pallas_call(
        functools.partial(chol_kernel, scale),
        out_shape=(jax.ShapeDtypeStruct((m, n), jnp.float32), jax.ShapeDtypeStruct((n, n), jnp.float32)),
        in_specs=[pl.BlockSpec(memory_space=pltpu.VMEM)] * 2,
        out_specs=(pl.BlockSpec(memory_space=pltpu.VMEM),) * 2,
        scratch_shapes=[pltpu.VMEM((n, n), jnp.float32), pltpu.VMEM((m, n), jnp.float32),
                        pltpu.VMEM((128, 128), jnp.float32), pltpu.VMEM((128, 128), jnp.float32),
                        pltpu.VMEM((128, 128), jnp.float32)],
        name="factor_solve",
    )(gram, rows)


def shifted(block, distance):
    count = lax.axis_size("col")
    return lax.ppermute(block, "col", [(i, (i + distance) % count) for i in range(count)])


def body(tile_values, tile_places, tile_counts, sketch):
    tile_stack = tile_values[0, 0]
    tile_size = tile_stack.shape[1]
    sketch_width = sketch.shape[1]
    row_devices = lax.axis_size("row")
    col_devices = lax.axis_size("col")
    local_rows = sketch.shape[0] // row_devices
    chunk_rows = local_rows // tile_size
    half = chunk_rows // 2
    panels = sketch.reshape(-1, tile_size, sketch_width)
    plan = make_plan(tile_places[0, 0], tile_counts, col_devices, chunk_rows)
    up, down = sparse_sum(plan, 0, tile_stack, panels, 0, (2, half))
    (later,) = sparse_sum(plan, 1, tile_stack, panels, chunk_rows, (1, chunk_rows * (col_devices - 1)))
    own, gram = ring_sum(shifted(up, 1), shifted(down, -1), later, (row_devices // 8, 4, col_devices))
    own_rows = own.reshape(local_rows, sketch_width)
    gram_blocks = gram.reshape(2, 5, 128, 128)
    order_scale = math.sqrt(local_rows * row_devices * col_devices)
    basis_rows, upper = chol_solve(gram_blocks, own_rows, order_scale)
    return basis_rows, upper


def solution(mesh):
    in_specs = (
        P("row", "col", None, None, None),
        P("row", "col", None, None),
        P("row", "col"),
        P("col", None),
    )
    out_specs = (P(("row", "col"), None), P())
    return jax.shard_map(body, mesh=mesh, in_specs=in_specs, out_specs=out_specs, check_vma=False)
```

```python
import functools, math
import jax
import jax.numpy as jnp
from jax import lax
from jax.experimental import pallas as pl
from jax.experimental.pallas import tpu as pltpu
from jax.sharding import PartitionSpec as P

GROUP = 4
TURN = 3
RING = 12
SPANS = 7 * 128

def sparse_kernel(base, stage, plan_ref, tiles, panels, *rest):
    nout = len(rest) - 6
    outs = rest[:nout]
    lhs, rhs, sums, tsem, psem, osem = rest[nout:]
    first = plan_ref[SPANS + stage]
    last = plan_ref[SPANS + stage + 1]
    size = tiles.shape[1]
    rows_each = outs[0].shape[0]
    spare = nout * rows_each

    def parts(g, k):
        word = plan_ref[g * GROUP + k]
        s = lax.rem(g, RING)
        live = word >= (1 << 23)
        tile = pltpu.make_async_copy(tiles.at[word & 511], lhs.at[s, :, pl.ds(k * size, size)], tsem.at[s, k])
        panel = pltpu.make_async_copy(panels.at[(word >> 9) & 511], rhs.at[s, pl.ds(k * size, size), :], psem.at[s, k])
        return live, tile, panel, s

    def issue(g):
        for k in range(GROUP):
            live, tile, panel, s = parts(g, k)
            @pl.when(live)
            def _():
                tile.start()
                panel.start()
            if k:
                @pl.when(jnp.logical_not(live))
                def _():
                    lhs[s, :, k * size:(k + 1) * size] = jnp.zeros((size, size), lhs.dtype)
                    rhs[s, k * size:(k + 1) * size, :] = jnp.zeros((size, rhs.shape[2]), rhs.dtype)

    def prime(g, c):
        issue(g)
        return c

    lax.fori_loop(first, jnp.minimum(first + RING - TURN, last), prime, 0)

    def clear(i, c):
        sums[i] = jnp.zeros(sums.shape[1:], sums.dtype)
        return c

    lax.fori_loop(0, sums.shape[0], clear, 0)

    def leave(p):
        for i, o in enumerate(outs):
            @pl.when(lax.div(p, rows_each) == i)
            def _():
                pltpu.make_async_copy(sums.at[p], o.at[p - i * rows_each], osem.at[p]).start()

    def leave_all(p, c):
        leave(p)
        return c

    def place_of(g):
        return ((plan_ref[jnp.minimum(g, last - 1) * GROUP] >> 18) & 31) - base

    def step(turn, done):
        g0 = first + turn * TURN
        for u in range(TURN):
            g = g0 + u
            @pl.when(g + RING - TURN < last)
            def _():
                issue(g + RING - TURN)
            @pl.when(g < last)
            def _():
                for k in range(GROUP):
                    live, tile, panel, s = parts(g, k)
                    @pl.when(live)
                    def _():
                        tile.wait()
                        panel.wait()
        ready = place_of(g0)
        lax.fori_loop(done, ready, leave_all, 0)
        for u in range(TURN):
            g = g0 + u
            s = lax.rem(g, RING)
            place = jnp.where(g < last, place_of(g), spare)
            prod = jnp.dot(lhs[s], rhs[s], preferred_element_type=jnp.float32)
            sums[place] = sums[place] + prod
        return ready

    done = lax.fori_loop(0, lax.div(last - first + TURN - 1, TURN), step, jnp.int32(0))
    lax.fori_loop(done, spare, leave_all, 0)

    def arrive(p, c):
        pltpu.make_async_copy(sums.at[p], outs[0].at[0], osem.at[p]).wait()
        return c

    lax.fori_loop(0, spare, arrive, 0)


def sparse_sum(plan, stage, tiles, panels, base, shape):
    nout, rows = shape
    width = panels.shape[2]
    size = tiles.shape[1]
    return pl.pallas_call(
        functools.partial(sparse_kernel, base, stage),
        grid_spec=pltpu.PrefetchScalarGridSpec(
            num_scalar_prefetch=1, grid=(),
            in_specs=[pl.BlockSpec(memory_space=pl.ANY)] * 2,
            out_specs=[pl.BlockSpec(memory_space=pl.ANY)] * nout,
            scratch_shapes=[pltpu.VMEM((RING, size, GROUP * size), tiles.dtype), pltpu.VMEM((RING, GROUP * size, width), panels.dtype),
                            pltpu.VMEM((nout * rows + 1, size, width), jnp.float32),
                            pltpu.SemaphoreType.DMA((RING, GROUP)), pltpu.SemaphoreType.DMA((RING, GROUP)), pltpu.SemaphoreType.DMA((nout * rows,))]),
        out_shape=[jax.ShapeDtypeStruct((rows, size, width), jnp.float32)] * nout,
        compiler_params=pltpu.CompilerParams(vmem_limit_bytes=67_000_000),
        cost_estimate=pl.CostEstimate(flops=2 * 360 * 128 * 128 * 512 * rows * nout // 24, bytes_accessed=50_000_000 * rows * nout // 24, transcendentals=0),
        name="tile_sums",
    )(plan, tiles, panels)

HI = lax.Precision.HIGHEST

def dot_hi(a, b, dims):
    return lax.dot_general(a, b, (dims, ((), ())), precision=HI, preferred_element_type=jnp.float32)

def plan_kernel(ncol, chunk, count_ref, places_ref, plan_ref, wide):
    me = lax.axis_index("col")
    width = wide.shape[1]
    wide[...] = jnp.zeros_like(wide)
    wide[:, :places_ref.shape[1]] = places_ref[...]
    rows = wide[0:1, :]
    cols = wide[1:2, :]
    ids = lax.broadcasted_iota(jnp.int32, (1, width), 1)
    live = ids < count_ref[0, 0]
    dest = jnp.zeros_like(rows)
    for q in range(1, ncol):
        dest = dest + (rows >= q * chunk).astype(jnp.int32)
    sub = rows - dest * chunk
    step = jnp.where(sub < chunk // 2, (me + 2 * ncol - 1 - dest) & (ncol - 1), (dest + 2 * ncol - 1 - me) & (ncol - 1))
    place = step * chunk + sub
    shelf = lax.broadcasted_iota(jnp.int32, (32, width), 0)
    held = jnp.where(shelf == jnp.where(live, place, 99), 1.0, 0.0)
    before = lax.broadcasted_iota(jnp.int32, (width, width), 0) < lax.broadcasted_iota(jnp.int32, (width, width), 1)
    rank = jnp.dot(held.astype(jnp.bfloat16), jnp.where(before, 1.0, 0.0).astype(jnp.bfloat16), preferred_element_type=jnp.float32)
    groups = (jnp.sum(held, axis=1, keepdims=True).astype(jnp.int32) + GROUP - 1) // GROUP
    wide_groups = jnp.broadcast_to(groups.astype(jnp.float32), (32, 128))
    under = lax.broadcasted_iota(jnp.int32, (32, 32), 1) < lax.broadcasted_iota(jnp.int32, (32, 32), 0)
    ahead = jnp.dot(jnp.where(under, 1.0, 0.0).astype(jnp.bfloat16), wide_groups.astype(jnp.bfloat16), preferred_element_type=jnp.float32)
    spot = jnp.sum(held * (rank + GROUP * ahead[:, 0:1]), axis=0, keepdims=True).astype(jnp.int32)
    spot = jnp.where(live, spot, -1)
    word = (ids + cols * 512 + place * (1 << 18) + (1 << 23)).astype(jnp.float32)
    high = jnp.where(lax.broadcasted_iota(jnp.int32, (8, width), 0) == (spot >> 7), word, 0.0)
    low = jnp.where(lax.broadcasted_iota(jnp.int32, (128, width), 0) == (spot & 127), 1.0, 0.0)
    plan = dot_hi(high, low, ((1,), (1,))).astype(jnp.int32)
    r8 = lax.broadcasted_iota(jnp.int32, (8, 128), 0)
    c8 = lax.broadcasted_iota(jnp.int32, (8, 128), 1)
    shelf8 = lax.broadcasted_iota(jnp.int32, (32, 128), 0)
    n0 = jnp.sum(jnp.where(shelf8 < chunk, wide_groups, 0.0), axis=0, keepdims=True).astype(jnp.int32)
    n1 = jnp.sum(wide_groups, axis=0, keepdims=True).astype(jnp.int32)
    plan_ref[...] = jnp.where(r8 == 7, jnp.where(c8 == 1, n0, jnp.where(c8 == 2, n1, 0)), plan)

def make_plan(places, count, ncol, chunk_rows):
    width = -(-places.shape[1] // 128) * 128
    return pl.pallas_call(
        functools.partial(plan_kernel, ncol, chunk_rows),
        out_shape=jax.ShapeDtypeStruct((8, 128), jnp.int32),
        in_specs=[pl.BlockSpec(memory_space=pltpu.SMEM), pl.BlockSpec(memory_space=pltpu.VMEM)],
        out_specs=pl.BlockSpec(memory_space=pltpu.VMEM),
        scratch_shapes=[pltpu.VMEM((2, width), jnp.int32)],
        name="tile_plan",
    )(count, places).reshape(8 * 128)


MESH = pl.DeviceIdType.MESH
BLOCKS = (((0, 0), (2, 2), (0, 1), (2, 3), (0, 2)), ((1, 1), (3, 3), (1, 2), (0, 3), (1, 3)))
SPOT = {ij: (h, b) for h in range(2) for b, ij in enumerate(BLOCKS[h])}

def ring_kernel(dims, up_ref, down_ref, later_ref, rows_ref, out_ref,
                head, later, box1, box2, part, mate, mine, inbox, tower, full,
                hsem, lsem, s1, r1, s2, r2, cs, cr, ps, pr, zs, zr, gs, gr, fs, fr):
    zn, xn, yn = dims
    row = lax.axis_index("row")
    y = lax.axis_index("col")
    core = lax.rem(row, 2)
    x = lax.rem(row // 2, xn)
    z = row // (2 * xn)
    other = 1 - core
    count = up_ref.shape[0]
    tall = up_ref.shape[1]

    def at(zz, xx, yy, cc):
        return ((zz * xn + xx) * 2 + cc, yy)

    partner = at(z, x, y, other)
    plane = []
    for j in range(1, xn * yn):
        dx, dy = j // yn, j % yn
        plane.append((at(z, lax.rem(x + dx, xn), lax.rem(y + dy, yn), core),
                      lax.rem(x + dx, xn) * yn + lax.rem(y + dy, yn),
                      lax.rem(x + xn - dx, xn) * yn + lax.rem(y + yn - dy, yn)))
    column = [at(lax.rem(z + j, zn), x, y, core) for j in range(1, zn)]
    own = x * yn + y
    piece = mine.shape[0] // (xn * yn)
    ring = [(row, lax.rem(y + 1, yn)), (row, lax.rem(y + yn - 1, yn))]

    barrier = pltpu.get_barrier_semaphore()
    peers = [partner] + [p[0] for p in plane] + column
    for peer in peers:
        pl.semaphore_signal(barrier, inc=1, device_id=peer, device_id_type=MESH)

    def remote(src, dst, send, recv, dev):
        return pltpu.make_async_remote_copy(src_ref=src, dst_ref=dst, send_sem=send, recv_sem=recv, device_id=dev, device_id_type=MESH)

    def head_copy(i, d):
        return pltpu.make_async_copy((up_ref, down_ref)[d].at[i], head.at[d, i], hsem.at[d, i])

    def later_copy(step, i, d):
        p = (2 * step + d) * count + i
        return pltpu.make_async_copy(later_ref.at[p], later.at[step, d, i], lsem.at[step, d, i])

    def hop1(i, d):
        return remote(head.at[d, i], box1.at[d, i], s1.at[d, i], r1.at[d, i], ring[d])

    def hop2(i, d):
        return remote(box1.at[d, i], box2.at[d, i], s2.at[d, i], r2.at[d, i], ring[d])

    for i in range(count):
        for d in range(2):
            head_copy(i, d).start()
            later_copy(0, i, d).start()
    for step in range(1, 3):
        for i in range(count):
            for d in range(2):
                later_copy(step, i, d).start()
    part[...] = jnp.zeros_like(part)
    pl.semaphore_wait(barrier, len(peers))

    def first(i, c):
        for d in range(2):
            head_copy(i, d).wait()
            later_copy(0, i, d).wait()
            head[d, i] = head[d, i] + later[0, d, i]
            hop1(i, d).start()
        return c

    lax.fori_loop(0, count, first, 0)

    def second(i, c):
        for d in range(2):
            later_copy(1, i, d).wait()
            hop1(i, d).wait_recv()
            box1[d, i] = box1[d, i] + later[1, d, i]
            hop2(i, d).start()
        return c

    lax.fori_loop(0, count, second, 0)

    def third(i, c):
        for d in range(2):
            later_copy(2, i, d).wait()
            hop2(i, d).wait_recv()
            total = box2[d, i] + later[2, d, i]
            rows_ref[d, i] = total
            for a in range(4):
                got = dot_hi(total[:, 128 * a:128 * a + 128], total[:, 128 * a:], ((0,), (0,)))
                for j in range(a, 4):
                    h, b = SPOT[a, j]
                    part[h, 128 * b:128 * b + 128, :] = part[h, 128 * b:128 * b + 128, :] + got[:, 128 * (j - a):128 * (j - a) + 128]
        return c

    lax.fori_loop(0, count, third, 0)

    swap = remote(part.at[other], mate, cs, cr, partner)
    swap.start()
    swap.wait_recv()
    mine[...] = part[core] + mate[...]
    order = sorted(range(len(plane)), key=lambda j: -(min((j + 1) // yn, xn - (j + 1) // yn) + min((j + 1) % yn, yn - (j + 1) % yn)))
    scatter = []
    for j in order:
        dev, theirs, _ = plane[j]
        c = remote(mine.at[pl.ds(pl.multiple_of(theirs * piece, 8), piece)], inbox.at[j], ps.at[j], pr.at[j], dev)
        c.start()
        scatter.append(c)
    total = mine[pl.ds(pl.multiple_of(own * piece, 8), piece), :]
    for j, c in zip(reversed(order), reversed(scatter)):
        c.wait_recv()
        total = total + inbox[j]
    tower[z] = total
    climb = []
    for j in sorted(range(zn - 1), key=lambda j: -min(j + 1, zn - j - 1)):
        c = remote(tower.at[z], tower.at[z], zs.at[j], zr.at[j], column[j])
        c.start()
        climb.append(c)
    for c in climb:
        c.wait_recv()
    total = tower[0]
    for k in range(1, zn):
        total = total + tower[k]
    full[core, own] = total
    spread = {}
    for j in order:
        dev, _, _ = plane[j]
        spread[j] = remote(full.at[core, own], full.at[core, own], gs.at[j], gr.at[j], dev)
        spread[j].start()
    hand = [remote(full.at[core, own], full.at[core, own], fs.at[len(plane)], fr.at[len(plane)], partner)]
    hand[0].start()
    for j in reversed(order):
        spread[j].wait_recv()
        source = plane[j][2]
        c = remote(full.at[core, source], full.at[core, source], fs.at[j], fr.at[j], partner)
        c.start()
        hand.append(c)
    for c in hand:
        c.wait_recv()
    out_ref[...] = full[...]
    for c in [swap] + scatter + climb + list(spread.values()) + hand:
        c.wait_send()

    def drain(i, c):
        for d in range(2):
            hop1(i, d).wait_send()
            hop2(i, d).wait_send()
        return c

    lax.fori_loop(0, count, drain, 0)

def ring_sum(up, down, later, dims):
    zn, xn, yn = dims
    count, tall, n = up.shape
    pieces = xn * yn
    deep = 5 * 128
    sem = pltpu.SemaphoreType.DMA
    f32 = jnp.float32
    return pl.pallas_call(
        functools.partial(ring_kernel, dims),
        out_shape=(jax.ShapeDtypeStruct((2, count, tall, n), f32), jax.ShapeDtypeStruct((2, pieces, deep // pieces, 128), f32)),
        in_specs=[pl.BlockSpec(memory_space=pl.ANY)] * 3,
        out_specs=(pl.BlockSpec(memory_space=pltpu.VMEM),) * 2,
        scratch_shapes=[pltpu.VMEM((2, count, tall, n), f32), pltpu.VMEM((3, 2, count, tall, n), f32),
                        pltpu.VMEM((2, count, tall, n), f32), pltpu.VMEM((2, count, tall, n), f32),
                        pltpu.VMEM((2, deep, 128), f32), pltpu.VMEM((deep, 128), f32), pltpu.VMEM((deep, 128), f32),
                        pltpu.VMEM((pieces - 1, deep // pieces, 128), f32), pltpu.VMEM((zn, deep // pieces, 128), f32),
                        pltpu.VMEM((2, pieces, deep // pieces, 128), f32),
                        sem((2, count)), sem((3, 2, count)), sem((2, count)), sem((2, count)), sem((2, count)), sem((2, count)),
                        sem, sem, sem((pieces - 1,)), sem((pieces - 1,)), sem((zn - 1,)), sem((zn - 1,)),
                        sem((pieces - 1,)), sem((pieces - 1,)), sem((pieces,)), sem((pieces,))],
        compiler_params=pltpu.CompilerParams(collective_id=0, has_side_effects=True, vmem_limit_bytes=67_000_000),
        name="ring_sum",
    )(up, down, later)


def factor_block(a_ref, w_ref, u_ref, c_ref):
    n = 128
    nv = n // 8
    lane = lax.broadcasted_iota(jnp.int32, (8, n), 1)
    sub = lax.broadcasted_iota(jnp.int32, (8, n), 0)
    a = [a_ref[8 * v:8 * v + 8, :] for v in range(nv)]
    b = [jnp.where(lane == sub + 8 * v, 1.0, 0.0).astype(jnp.float32) for v in range(nv)]
    for r in range(nv):
        col = {}
        for v in range(r, nv):
            for k in range(8):
                col[k, v] = jnp.broadcast_to(a[v][:, 8 * r + k:8 * r + k + 1], (8, n))
        for k in range(8):
            c_ref[r, 8 * k:8 * k + 8, :] = col[k, r]
        e = {}
        for k in range(8):
            for j in range(k, 8):
                e[k, j] = c_ref[r, pl.ds(8 * j + k, 8, stride=0), :]
        c_ref[r, 64:72, :] = a[r]
        c_ref[r, 72:80, :] = b[r]
        ra = [c_ref[r, pl.ds(64 + k, 8, stride=0), :] for k in range(8)]
        rb = [c_ref[r, pl.ds(72 + k, 8, stride=0), :] for k in range(8)]
        for k in range(8):
            rs = lax.rsqrt(e[k, k])
            for j in range(k + 1, 8):
                e[k, j] = e[k, j] * rs
            for i in range(k + 1, 8):
                for j in range(i, 8):
                    e[i, j] = e[i, j] - e[k, i] * e[k, j]
            ra[k] = ra[k] * rs
            rb[k] = rb[k] * rs
            for j in range(k + 1, 8):
                ra[j] = ra[j] - e[k, j] * ra[k]
                rb[j] = rb[j] - e[k, j] * rb[k]
            for v in range(r + 1, nv):
                col[k, v] = col[k, v] * rs
                for j in range(k + 1, 8):
                    col[j, v] = col[j, v] - e[k, j] * col[k, v]
                a[v] = a[v] - col[k, v] * ra[k]
                b[v] = b[v] - col[k, v] * rb[k]
        ua, ub = ra[0], rb[0]
        for k in range(1, 8):
            ua = jnp.where(sub == k, ra[k], ua)
            ub = jnp.where(sub == k, rb[k], ub)
        u_ref[8 * r:8 * r + 8, :] = jnp.where(lane >= sub + 8 * r, ua, 0.0)
        w_ref[8 * r:8 * r + 8, :] = ub

def chol_kernel(scale, g_ref, s_ref, x_ref, t_ref, gw, xs, d_ref, w_ref, u_ref, c_ref):
    n = gw.shape[0]
    nb = n // 128
    for h in range(2):
        for b, (i, j) in enumerate(BLOCKS[h]):
            gw[128 * i:128 * i + 128, 128 * j:128 * j + 128] = g_ref[h, b]
    xs[...] = s_ref[...] * scale
    t_ref[...] = jnp.zeros_like(t_ref)
    for k in range(nb):
        lo = 128 * k
        hi = lo + 128
        d_ref[...] = gw[lo:hi, lo:hi]
        factor_block(d_ref, w_ref, u_ref, c_ref)
        w = w_ref[...]
        t_ref[lo:hi, lo:hi] = u_ref[...] * (1.0 / scale)
        if hi < n:
            up = dot_hi(w, gw[lo:hi, hi:n], ((1,), (0,)))
            t_ref[lo:hi, hi:n] = up * (1.0 / scale)
            for i in range(hi, n, 128):
                gw[i:i + 128, i:n] = gw[i:i + 128, i:n] - dot_hi(up[:, i - hi:i - hi + 128], up[:, i - hi:], ((0,), (0,)))
        xk = dot_hi(xs[:, lo:hi], w, ((1,), (1,)))
        x_ref[:, lo:hi] = xk
        if hi < n:
            xs[:, hi:n] = xs[:, hi:n] - dot_hi(xk, up, ((1,), (0,)))


def chol_solve(gram, rows, scale):
    m, n = rows.shape
    return pl.pallas_call(
        functools.partial(chol_kernel, scale),
        out_shape=(jax.ShapeDtypeStruct((m, n), jnp.float32), jax.ShapeDtypeStruct((n, n), jnp.float32)),
        in_specs=[pl.BlockSpec(memory_space=pltpu.VMEM)] * 2,
        out_specs=(pl.BlockSpec(memory_space=pltpu.VMEM),) * 2,
        scratch_shapes=[pltpu.VMEM((n, n), jnp.float32), pltpu.VMEM((m, n), jnp.float32),
                        pltpu.VMEM((128, 128), jnp.float32), pltpu.VMEM((128, 128), jnp.float32),
                        pltpu.VMEM((128, 128), jnp.float32), pltpu.VMEM((16, 80, 128), jnp.float32)],
        name="factor_solve",
    )(gram, rows)


def shifted(block, distance):
    count = lax.axis_size("col")
    return lax.ppermute(block, "col", [(i, (i + distance) % count) for i in range(count)])


def body(tile_values, tile_places, tile_counts, sketch):
    tile_stack = tile_values[0, 0]
    tile_size = tile_stack.shape[1]
    sketch_width = sketch.shape[1]
    row_devices = lax.axis_size("row")
    col_devices = lax.axis_size("col")
    local_rows = sketch.shape[0] // row_devices
    chunk_rows = local_rows // tile_size
    half = chunk_rows // 2
    panels = sketch.reshape(-1, tile_size, sketch_width)
    plan = make_plan(tile_places[0, 0], tile_counts, col_devices, chunk_rows)
    up, down = sparse_sum(plan, 0, tile_stack, panels, 0, (2, half))
    (later,) = sparse_sum(plan, 1, tile_stack, panels, chunk_rows, (1, chunk_rows * (col_devices - 1)))
    own, gram = ring_sum(shifted(up, 1), shifted(down, -1), later, (row_devices // 8, 4, col_devices))
    own_rows = own.reshape(local_rows, sketch_width)
    gram_blocks = gram.reshape(2, 5, 128, 128)
    order_scale = math.sqrt(local_rows * row_devices * col_devices)
    basis_rows, upper = chol_solve(gram_blocks, own_rows, order_scale)
    return basis_rows, upper


def solution(mesh):
    in_specs = (
        P("row", "col", None, None, None),
        P("row", "col", None, None),
        P("row", "col"),
        P("col", None),
    )
    out_specs = (P(("row", "col"), None), P())
    return jax.shard_map(body, mesh=mesh, in_specs=in_specs, out_specs=out_specs, check_vma=False)
```

```python
import functools, math
import jax
import jax.numpy as jnp
from jax import lax
from jax.experimental import pallas as pl
from jax.experimental.pallas import tpu as pltpu
from jax.sharding import PartitionSpec as P

GROUP = 4
TURN = 6
RING = 18
SPANS = 7 * 128

def sparse_kernel(base, stage, plan_ref, tiles, panels, *rest):
    nout = len(rest) - 6
    outs = rest[:nout]
    lhs, rhs, sums, tsem, psem, osem = rest[nout:]
    first = plan_ref[SPANS + stage]
    last = plan_ref[SPANS + stage + 1]
    size = tiles.shape[1]
    rows_each = outs[0].shape[0]
    spare = nout * rows_each

    def parts(g, k):
        word = plan_ref[g * GROUP + k]
        s = lax.rem(g, RING)
        live = word >= (1 << 23)
        tile = pltpu.make_async_copy(tiles.at[word & 511], lhs.at[s, :, pl.ds(k * size, size)], tsem.at[s])
        panel = pltpu.make_async_copy(panels.at[(word >> 9) & 511], rhs.at[s, pl.ds(k * size, size), :], psem.at[s])
        return live, tile, panel, s

    def is_full(g):
        return plan_ref[g * GROUP + GROUP - 1] >= (1 << 23)

    def issue(g):
        full = is_full(g)
        @pl.when(full)
        def _():
            for k in range(GROUP):
                live, tile, panel, s = parts(g, k)
                panel.start()
                tile.start()
        @pl.when(jnp.logical_not(full))
        def _():
            for k in range(GROUP):
                live, tile, panel, s = parts(g, k)
                @pl.when(live)
                def _():
                    panel.start()
                    tile.start()
                if k:
                    @pl.when(jnp.logical_not(live))
                    def _():
                        lhs[s, :, k * size:(k + 1) * size] = jnp.zeros((size, size), lhs.dtype)
                        rhs[s, k * size:(k + 1) * size, :] = jnp.zeros((size, rhs.shape[2]), rhs.dtype)

    def settle(g):
        full = is_full(g)
        @pl.when(full)
        def _():
            s = lax.rem(g, RING)
            pltpu.make_async_copy(lhs.at[s], lhs.at[s], tsem.at[s]).wait()
            pltpu.make_async_copy(rhs.at[s], rhs.at[s], psem.at[s]).wait()
        @pl.when(jnp.logical_not(full))
        def _():
            for k in range(GROUP):
                live, tile, panel, s = parts(g, k)
                @pl.when(live)
                def _():
                    tile.wait()
                    panel.wait()

    def prime(g, c):
        issue(g)
        return c

    lax.fori_loop(first, jnp.minimum(first + RING - TURN, last), prime, 0)

    def clear(i, c):
        sums[i] = jnp.zeros(sums.shape[1:], sums.dtype)
        return c

    lax.fori_loop(0, sums.shape[0], clear, 0)

    def leave(p):
        for i, o in enumerate(outs):
            @pl.when(lax.div(p, rows_each) == i)
            def _():
                pltpu.make_async_copy(sums.at[p], o.at[p - i * rows_each], osem.at[p]).start()

    def leave_all(p, c):
        leave(p)
        return c

    def place_of(g):
        return ((plan_ref[jnp.minimum(g, last - 1) * GROUP] >> 18) & 31) - base

    def step(turn, done):
        g0 = first + turn * TURN
        for u in range(TURN):
            g = g0 + u
            @pl.when(g + RING - TURN < last)
            def _():
                issue(g + RING - TURN)
            @pl.when(g < last)
            def _():
                settle(g)
        ready = place_of(g0)
        lax.fori_loop(done, ready, leave_all, 0)
        for u in range(TURN):
            g = g0 + u
            s = lax.rem(g, RING)
            place = jnp.where(g < last, place_of(g), spare)
            prod = jnp.dot(lhs[s], rhs[s], preferred_element_type=jnp.float32)
            sums[place] = sums[place] + prod
        return ready

    done = lax.fori_loop(0, lax.div(last - first + TURN - 1, TURN), step, jnp.int32(0))
    lax.fori_loop(done, spare, leave_all, 0)

    def arrive(p, c):
        pltpu.make_async_copy(sums.at[p], outs[0].at[0], osem.at[p]).wait()
        return c

    lax.fori_loop(0, spare, arrive, 0)


def sparse_sum(plan, stage, tiles, panels, base, shape):
    nout, rows = shape
    width = panels.shape[2]
    size = tiles.shape[1]
    return pl.pallas_call(
        functools.partial(sparse_kernel, base, stage),
        grid_spec=pltpu.PrefetchScalarGridSpec(
            num_scalar_prefetch=1, grid=(),
            in_specs=[pl.BlockSpec(memory_space=pl.ANY)] * 2,
            out_specs=[pl.BlockSpec(memory_space=pl.ANY)] * nout,
            scratch_shapes=[pltpu.VMEM((RING, size, GROUP * size), tiles.dtype), pltpu.VMEM((RING, GROUP * size, width), panels.dtype),
                            pltpu.VMEM((nout * rows + 1, size, width), jnp.float32),
                            pltpu.SemaphoreType.DMA((RING,)), pltpu.SemaphoreType.DMA((RING,)), pltpu.SemaphoreType.DMA((nout * rows,))]),
        out_shape=[jax.ShapeDtypeStruct((rows, size, width), jnp.float32)] * nout,
        compiler_params=pltpu.CompilerParams(vmem_limit_bytes=67_000_000),
        cost_estimate=pl.CostEstimate(flops=2 * 360 * 128 * 128 * 512 * rows * nout // 24, bytes_accessed=50_000_000 * rows * nout // 24, transcendentals=0),
        name="tile_sums",
    )(plan, tiles, panels)

HI = lax.Precision.HIGHEST

def dot_hi(a, b, dims):
    return lax.dot_general(a, b, (dims, ((), ())), precision=HI, preferred_element_type=jnp.float32)

def plan_kernel(ncol, chunk, count_ref, places_ref, plan_ref, wide):
    me = lax.axis_index("col")
    width = wide.shape[1]
    wide[...] = jnp.zeros_like(wide)
    wide[:, :places_ref.shape[1]] = places_ref[...]
    rows = wide[0:1, :]
    cols = wide[1:2, :]
    ids = lax.broadcasted_iota(jnp.int32, (1, width), 1)
    live = ids < count_ref[0, 0]
    dest = jnp.zeros_like(rows)
    for q in range(1, ncol):
        dest = dest + (rows >= q * chunk).astype(jnp.int32)
    sub = rows - dest * chunk
    step = jnp.where(sub < chunk // 2, (me + 2 * ncol - 1 - dest) & (ncol - 1), (dest + 2 * ncol - 1 - me) & (ncol - 1))
    place = step * chunk + sub
    shelf = lax.broadcasted_iota(jnp.int32, (32, width), 0)
    held = jnp.where(shelf == jnp.where(live, place, 99), 1.0, 0.0)
    before = lax.broadcasted_iota(jnp.int32, (width, width), 0) < lax.broadcasted_iota(jnp.int32, (width, width), 1)
    rank = jnp.dot(held.astype(jnp.bfloat16), jnp.where(before, 1.0, 0.0).astype(jnp.bfloat16), preferred_element_type=jnp.float32)
    groups = (jnp.sum(held, axis=1, keepdims=True).astype(jnp.int32) + GROUP - 1) // GROUP
    wide_groups = jnp.broadcast_to(groups.astype(jnp.float32), (32, 128))
    under = lax.broadcasted_iota(jnp.int32, (32, 32), 1) < lax.broadcasted_iota(jnp.int32, (32, 32), 0)
    ahead = jnp.dot(jnp.where(under, 1.0, 0.0).astype(jnp.bfloat16), wide_groups.astype(jnp.bfloat16), preferred_element_type=jnp.float32)
    spot = jnp.sum(held * (rank + GROUP * ahead[:, 0:1]), axis=0, keepdims=True).astype(jnp.int32)
    spot = jnp.where(live, spot, -1)
    word = (ids + cols * 512 + place * (1 << 18) + (1 << 23)).astype(jnp.float32)
    high = jnp.where(lax.broadcasted_iota(jnp.int32, (8, width), 0) == (spot >> 7), word, 0.0)
    low = jnp.where(lax.broadcasted_iota(jnp.int32, (128, width), 0) == (spot & 127), 1.0, 0.0)
    plan = dot_hi(high, low, ((1,), (1,))).astype(jnp.int32)
    r8 = lax.broadcasted_iota(jnp.int32, (8, 128), 0)
    c8 = lax.broadcasted_iota(jnp.int32, (8, 128), 1)
    shelf8 = lax.broadcasted_iota(jnp.int32, (32, 128), 0)
    n0 = jnp.sum(jnp.where(shelf8 < chunk, wide_groups, 0.0), axis=0, keepdims=True).astype(jnp.int32)
    n1 = jnp.sum(wide_groups, axis=0, keepdims=True).astype(jnp.int32)
    plan_ref[...] = jnp.where(r8 == 7, jnp.where(c8 == 1, n0, jnp.where(c8 == 2, n1, 0)), plan)

def make_plan(places, count, ncol, chunk_rows):
    width = -(-places.shape[1] // 128) * 128
    return pl.pallas_call(
        functools.partial(plan_kernel, ncol, chunk_rows),
        out_shape=jax.ShapeDtypeStruct((8, 128), jnp.int32),
        in_specs=[pl.BlockSpec(memory_space=pltpu.SMEM), pl.BlockSpec(memory_space=pltpu.VMEM)],
        out_specs=pl.BlockSpec(memory_space=pltpu.VMEM),
        scratch_shapes=[pltpu.VMEM((2, width), jnp.int32)],
        name="tile_plan",
    )(count, places).reshape(8 * 128)


MESH = pl.DeviceIdType.MESH
BLOCKS = (((0, 0), (2, 2), (0, 1), (2, 3), (0, 2)), ((1, 1), (3, 3), (1, 2), (0, 3), (1, 3)))
SPOT = {ij: (h, b) for h in range(2) for b, ij in enumerate(BLOCKS[h])}

def ring_kernel(dims, up_ref, down_ref, later_ref, rows_ref, out_ref,
                head, later, box1, box2, part, mate, mine, inbox, tower, full,
                hsem, lsem, s1, r1, s2, r2, cs, cr, ps, pr, zs, zr, gs, gr, fs, fr):
    zn, xn, yn = dims
    row = lax.axis_index("row")
    y = lax.axis_index("col")
    core = lax.rem(row, 2)
    x = lax.rem(row // 2, xn)
    z = row // (2 * xn)
    other = 1 - core
    count = up_ref.shape[0]
    tall = up_ref.shape[1]

    def at(zz, xx, yy, cc):
        return ((zz * xn + xx) * 2 + cc, yy)

    partner = at(z, x, y, other)
    plane = []
    for j in range(1, xn * yn):
        dx, dy = j // yn, j % yn
        plane.append((at(z, lax.rem(x + dx, xn), lax.rem(y + dy, yn), core),
                      lax.rem(x + dx, xn) * yn + lax.rem(y + dy, yn),
                      lax.rem(x + xn - dx, xn) * yn + lax.rem(y + yn - dy, yn)))
    column = [at(lax.rem(z + j, zn), x, y, core) for j in range(1, zn)]
    own = x * yn + y
    piece = mine.shape[0] // (xn * yn)
    ring = [(row, lax.rem(y + 1, yn)), (row, lax.rem(y + yn - 1, yn))]

    barrier = pltpu.get_barrier_semaphore()
    peers = [partner] + [p[0] for p in plane] + column
    for peer in peers:
        pl.semaphore_signal(barrier, inc=1, device_id=peer, device_id_type=MESH)

    def remote(src, dst, send, recv, dev):
        return pltpu.make_async_remote_copy(src_ref=src, dst_ref=dst, send_sem=send, recv_sem=recv, device_id=dev, device_id_type=MESH)

    def head_copy(i, d):
        return pltpu.make_async_copy((up_ref, down_ref)[d].at[i], head.at[d, i], hsem.at[d, i])

    def later_copy(step, i, d):
        p = (2 * step + d) * count + i
        return pltpu.make_async_copy(later_ref.at[p], later.at[step, d, i], lsem.at[step, d, i])

    def hop1(i, d):
        return remote(head.at[d, i], box1.at[d, i], s1.at[d, i], r1.at[d, i], ring[d])

    def hop2(i, d):
        return remote(box1.at[d, i], box2.at[d, i], s2.at[d, i], r2.at[d, i], ring[d])

    for i in range(count):
        for d in range(2):
            head_copy(i, d).start()
            later_copy(0, i, d).start()
    for step in range(1, 3):
        for i in range(count):
            for d in range(2):
                later_copy(step, i, d).start()
    part[...] = jnp.zeros_like(part)
    pl.semaphore_wait(barrier, len(peers))

    def first(i, c):
        for d in range(2):
            head_copy(i, d).wait()
            later_copy(0, i, d).wait()
            head[d, i] = head[d, i] + later[0, d, i]
            hop1(i, d).start()
        return c

    lax.fori_loop(0, count, first, 0)

    def second(i, c):
        for d in range(2):
            later_copy(1, i, d).wait()
            hop1(i, d).wait_recv()
            box1[d, i] = box1[d, i] + later[1, d, i]
            hop2(i, d).start()
        return c

    lax.fori_loop(0, count, second, 0)

    def third(i, c):
        for d in range(2):
            later_copy(2, i, d).wait()
            hop2(i, d).wait_recv()
            total = box2[d, i] + later[2, d, i]
            rows_ref[d, i] = total
            for a in range(4):
                got = dot_hi(total[:, 128 * a:128 * a + 128], total[:, 128 * a:], ((0,), (0,)))
                for j in range(a, 4):
                    h, b = SPOT[a, j]
                    part[h, 128 * b:128 * b + 128, :] = part[h, 128 * b:128 * b + 128, :] + got[:, 128 * (j - a):128 * (j - a) + 128]
        return c

    lax.fori_loop(0, count, third, 0)

    swap = remote(part.at[other], mate, cs, cr, partner)
    swap.start()
    swap.wait_recv()
    mine[...] = part[core] + mate[...]
    order = sorted(range(len(plane)), key=lambda j: -(min((j + 1) // yn, xn - (j + 1) // yn) + min((j + 1) % yn, yn - (j + 1) % yn)))
    scatter = []
    for j in order:
        dev, theirs, _ = plane[j]
        c = remote(mine.at[pl.ds(pl.multiple_of(theirs * piece, 8), piece)], inbox.at[j], ps.at[j], pr.at[j], dev)
        c.start()
        scatter.append(c)
    total = mine[pl.ds(pl.multiple_of(own * piece, 8), piece), :]
    for j, c in zip(reversed(order), reversed(scatter)):
        c.wait_recv()
        total = total + inbox[j]
    tower[z] = total
    climb = []
    for j in sorted(range(zn - 1), key=lambda j: -min(j + 1, zn - j - 1)):
        c = remote(tower.at[z], tower.at[z], zs.at[j], zr.at[j], column[j])
        c.start()
        climb.append(c)
    for c in climb:
        c.wait_recv()
    total = tower[0]
    for k in range(1, zn):
        total = total + tower[k]
    full[core, own] = total
    spread = {}
    for j in order:
        dev, _, _ = plane[j]
        spread[j] = remote(full.at[core, own], full.at[core, own], gs.at[j], gr.at[j], dev)
        spread[j].start()
    hand = [remote(full.at[core, own], full.at[core, own], fs.at[len(plane)], fr.at[len(plane)], partner)]
    hand[0].start()
    for j in reversed(order):
        spread[j].wait_recv()
        source = plane[j][2]
        c = remote(full.at[core, source], full.at[core, source], fs.at[j], fr.at[j], partner)
        c.start()
        hand.append(c)
    for c in hand:
        c.wait_recv()
    out_ref[...] = full[...]
    for c in [swap] + scatter + climb + list(spread.values()) + hand:
        c.wait_send()

    def drain(i, c):
        for d in range(2):
            hop1(i, d).wait_send()
            hop2(i, d).wait_send()
        return c

    lax.fori_loop(0, count, drain, 0)

def ring_sum(up, down, later, dims):
    zn, xn, yn = dims
    count, tall, n = up.shape
    pieces = xn * yn
    deep = 5 * 128
    sem = pltpu.SemaphoreType.DMA
    f32 = jnp.float32
    return pl.pallas_call(
        functools.partial(ring_kernel, dims),
        out_shape=(jax.ShapeDtypeStruct((2, count, tall, n), f32), jax.ShapeDtypeStruct((2, pieces, deep // pieces, 128), f32)),
        in_specs=[pl.BlockSpec(memory_space=pl.ANY)] * 3,
        out_specs=(pl.BlockSpec(memory_space=pltpu.VMEM),) * 2,
        scratch_shapes=[pltpu.VMEM((2, count, tall, n), f32), pltpu.VMEM((3, 2, count, tall, n), f32),
                        pltpu.VMEM((2, count, tall, n), f32), pltpu.VMEM((2, count, tall, n), f32),
                        pltpu.VMEM((2, deep, 128), f32), pltpu.VMEM((deep, 128), f32), pltpu.VMEM((deep, 128), f32),
                        pltpu.VMEM((pieces - 1, deep // pieces, 128), f32), pltpu.VMEM((zn, deep // pieces, 128), f32),
                        pltpu.VMEM((2, pieces, deep // pieces, 128), f32),
                        sem((2, count)), sem((3, 2, count)), sem((2, count)), sem((2, count)), sem((2, count)), sem((2, count)),
                        sem, sem, sem((pieces - 1,)), sem((pieces - 1,)), sem((zn - 1,)), sem((zn - 1,)),
                        sem((pieces - 1,)), sem((pieces - 1,)), sem((pieces,)), sem((pieces,))],
        compiler_params=pltpu.CompilerParams(collective_id=0, has_side_effects=True, vmem_limit_bytes=67_000_000),
        name="ring_sum",
    )(up, down, later)


def factor_block(a_ref, w_ref, u_ref, c_ref):
    n = 128
    nv = n // 8
    lane = lax.broadcasted_iota(jnp.int32, (8, n), 1)
    sub = lax.broadcasted_iota(jnp.int32, (8, n), 0)
    a = [a_ref[8 * v:8 * v + 8, :] for v in range(nv)]
    b = [jnp.where(lane == sub + 8 * v, 1.0, 0.0).astype(jnp.float32) for v in range(nv)]
    for r in range(nv):
        col = {}
        for v in range(r, nv):
            for k in range(8):
                col[k, v] = jnp.broadcast_to(a[v][:, 8 * r + k:8 * r + k + 1], (8, n))
        for k in range(8):
            c_ref[r, 8 * k:8 * k + 8, :] = col[k, r]
        e = {}
        for k in range(8):
            for j in range(k, 8):
                e[k, j] = c_ref[r, pl.ds(8 * j + k, 8, stride=0), :]
        c_ref[r, 64:72, :] = a[r]
        c_ref[r, 72:80, :] = b[r]
        ra = [c_ref[r, pl.ds(64 + k, 8, stride=0), :] for k in range(8)]
        rb = [c_ref[r, pl.ds(72 + k, 8, stride=0), :] for k in range(8)]
        for k in range(8):
            rs = lax.rsqrt(e[k, k])
            for j in range(k + 1, 8):
                e[k, j] = e[k, j] * rs
            for i in range(k + 1, 8):
                for j in range(i, 8):
                    e[i, j] = e[i, j] - e[k, i] * e[k, j]
            ra[k] = ra[k] * rs
            rb[k] = rb[k] * rs
            for j in range(k + 1, 8):
                ra[j] = ra[j] - e[k, j] * ra[k]
                rb[j] = rb[j] - e[k, j] * rb[k]
            for v in range(r + 1, nv):
                col[k, v] = col[k, v] * rs
                for j in range(k + 1, 8):
                    col[j, v] = col[j, v] - e[k, j] * col[k, v]
                a[v] = a[v] - col[k, v] * ra[k]
                b[v] = b[v] - col[k, v] * rb[k]
        ua, ub = ra[0], rb[0]
        for k in range(1, 8):
            ua = jnp.where(sub == k, ra[k], ua)
            ub = jnp.where(sub == k, rb[k], ub)
        u_ref[8 * r:8 * r + 8, :] = jnp.where(lane >= sub + 8 * r, ua, 0.0)
        w_ref[8 * r:8 * r + 8, :] = ub

def chol_kernel(scale, g_ref, s_ref, x_ref, t_ref, gw, xs, d_ref, w_ref, u_ref, c_ref):
    n = gw.shape[0]
    nb = n // 128
    for h in range(2):
        for b, (i, j) in enumerate(BLOCKS[h]):
            gw[128 * i:128 * i + 128, 128 * j:128 * j + 128] = g_ref[h, b]
    xs[...] = s_ref[...] * scale
    t_ref[...] = jnp.zeros_like(t_ref)
    for k in range(nb):
        lo = 128 * k
        hi = lo + 128
        d_ref[...] = gw[lo:hi, lo:hi]
        factor_block(d_ref, w_ref, u_ref, c_ref)
        w = w_ref[...]
        t_ref[lo:hi, lo:hi] = u_ref[...] * (1.0 / scale)
        if hi < n:
            up = dot_hi(w, gw[lo:hi, hi:n], ((1,), (0,)))
            t_ref[lo:hi, hi:n] = up * (1.0 / scale)
            for i in range(hi, n, 128):
                gw[i:i + 128, i:n] = gw[i:i + 128, i:n] - dot_hi(up[:, i - hi:i - hi + 128], up[:, i - hi:], ((0,), (0,)))
        xk = dot_hi(xs[:, lo:hi], w, ((1,), (1,)))
        x_ref[:, lo:hi] = xk
        if hi < n:
            xs[:, hi:n] = xs[:, hi:n] - dot_hi(xk, up, ((1,), (0,)))


def chol_solve(gram, rows, scale):
    m, n = rows.shape
    return pl.pallas_call(
        functools.partial(chol_kernel, scale),
        out_shape=(jax.ShapeDtypeStruct((m, n), jnp.float32), jax.ShapeDtypeStruct((n, n), jnp.float32)),
        in_specs=[pl.BlockSpec(memory_space=pltpu.VMEM)] * 2,
        out_specs=(pl.BlockSpec(memory_space=pltpu.VMEM),) * 2,
        scratch_shapes=[pltpu.VMEM((n, n), jnp.float32), pltpu.VMEM((m, n), jnp.float32),
                        pltpu.VMEM((128, 128), jnp.float32), pltpu.VMEM((128, 128), jnp.float32),
                        pltpu.VMEM((128, 128), jnp.float32), pltpu.VMEM((16, 80, 128), jnp.float32)],
        name="factor_solve",
    )(gram, rows)


def shifted(block, distance):
    count = lax.axis_size("col")
    return lax.ppermute(block, "col", [(i, (i + distance) % count) for i in range(count)])


def body(tile_values, tile_places, tile_counts, sketch):
    tile_stack = tile_values[0, 0]
    tile_size = tile_stack.shape[1]
    sketch_width = sketch.shape[1]
    row_devices = lax.axis_size("row")
    col_devices = lax.axis_size("col")
    local_rows = sketch.shape[0] // row_devices
    chunk_rows = local_rows // tile_size
    half = chunk_rows // 2
    panels = sketch.reshape(-1, tile_size, sketch_width)
    plan = make_plan(tile_places[0, 0], tile_counts, col_devices, chunk_rows)
    up, down = sparse_sum(plan, 0, tile_stack, panels, 0, (2, half))
    (later,) = sparse_sum(plan, 1, tile_stack, panels, chunk_rows, (1, chunk_rows * (col_devices - 1)))
    own, gram = ring_sum(shifted(up, 1), shifted(down, -1), later, (row_devices // 8, 4, col_devices))
    own_rows = own.reshape(local_rows, sketch_width)
    gram_blocks = gram.reshape(2, 5, 128, 128)
    order_scale = math.sqrt(local_rows * row_devices * col_devices)
    basis_rows, upper = chol_solve(gram_blocks, own_rows, order_scale)
    return basis_rows, upper


def solution(mesh):
    in_specs = (
        P("row", "col", None, None, None),
        P("row", "col", None, None),
        P("row", "col"),
        P("col", None),
    )
    out_specs = (P(("row", "col"), None), P())
    return jax.shard_map(body, mesh=mesh, in_specs=in_specs, out_specs=out_specs, check_vma=False)
```

```python
import functools, math
import jax
import jax.numpy as jnp
from jax import lax
from jax.experimental import pallas as pl
from jax.experimental.pallas import tpu as pltpu
from jax.sharding import PartitionSpec as P

GROUP = 4
TURN = 6
RING = 18
SPANS = 7 * 128

def sparse_kernel(base, stage, plan_ref, tiles, panels, *rest):
    nout = len(rest) - 6
    outs = rest[:nout]
    lhs, rhs, sums, tsem, psem, osem = rest[nout:]
    first = plan_ref[SPANS + stage]
    last = plan_ref[SPANS + stage + 1]
    size = tiles.shape[1]
    rows_each = outs[0].shape[0]
    spare = nout * rows_each

    def parts(g, k):
        word = plan_ref[g * GROUP + k]
        s = lax.rem(g, RING)
        live = word >= (1 << 23)
        tile = pltpu.make_async_copy(tiles.at[word & 511], lhs.at[s, :, pl.ds(k * size, size)], tsem.at[s])
        panel = pltpu.make_async_copy(panels.at[(word >> 9) & 511], rhs.at[s, pl.ds(k * size, size), :], psem.at[s])
        return live, tile, panel, s

    def is_full(g):
        return plan_ref[g * GROUP + GROUP - 1] >= (1 << 23)

    def issue(g):
        full = is_full(g)
        @pl.when(full)
        def _():
            for k in range(GROUP):
                live, tile, panel, s = parts(g, k)
                panel.start()
                tile.start()
        @pl.when(jnp.logical_not(full))
        def _():
            for k in range(GROUP):
                live, tile, panel, s = parts(g, k)
                @pl.when(live)
                def _():
                    panel.start()
                    tile.start()
                if k:
                    @pl.when(jnp.logical_not(live))
                    def _():
                        lhs[s, :, k * size:(k + 1) * size] = jnp.zeros((size, size), lhs.dtype)
                        rhs[s, k * size:(k + 1) * size, :] = jnp.zeros((size, rhs.shape[2]), rhs.dtype)

    def settle(g):
        full = is_full(g)
        @pl.when(full)
        def _():
            s = lax.rem(g, RING)
            pltpu.make_async_copy(lhs.at[s], lhs.at[s], tsem.at[s]).wait()
            pltpu.make_async_copy(rhs.at[s], rhs.at[s], psem.at[s]).wait()
        @pl.when(jnp.logical_not(full))
        def _():
            for k in range(GROUP):
                live, tile, panel, s = parts(g, k)
                @pl.when(live)
                def _():
                    tile.wait()
                    panel.wait()

    def prime(g, c):
        issue(g)
        return c

    lax.fori_loop(first, jnp.minimum(first + RING - TURN, last), prime, 0)

    def clear(i, c):
        sums[i] = jnp.zeros(sums.shape[1:], sums.dtype)
        return c

    lax.fori_loop(0, sums.shape[0], clear, 0)

    def leave(p):
        for i, o in enumerate(outs):
            @pl.when(lax.div(p, rows_each) == i)
            def _():
                pltpu.make_async_copy(sums.at[p], o.at[p - i * rows_each], osem.at[p]).start()

    def leave_all(p, c):
        leave(p)
        return c

    def place_of(g):
        return ((plan_ref[jnp.minimum(g, last - 1) * GROUP] >> 18) & 31) - base

    def step(turn, done):
        g0 = first + turn * TURN
        for u in range(TURN):
            g = g0 + u
            @pl.when(g + RING - TURN < last)
            def _():
                issue(g + RING - TURN)
            @pl.when(g < last)
            def _():
                settle(g)
        ready = place_of(g0)
        lax.fori_loop(done, ready, leave_all, 0)
        for u in range(TURN):
            g = g0 + u
            s = lax.rem(g, RING)
            place = jnp.where(g < last, place_of(g), spare)
            prod = jnp.dot(lhs[s], rhs[s], preferred_element_type=jnp.float32)
            sums[place] = sums[place] + prod
        return ready

    done = lax.fori_loop(0, lax.div(last - first + TURN - 1, TURN), step, jnp.int32(0))
    lax.fori_loop(done, spare, leave_all, 0)

    def arrive(p, c):
        pltpu.make_async_copy(sums.at[p], outs[0].at[0], osem.at[p]).wait()
        return c

    lax.fori_loop(0, spare, arrive, 0)


def sparse_sum(plan, stage, tiles, panels, base, shape):
    nout, rows = shape
    width = panels.shape[2]
    size = tiles.shape[1]
    return pl.pallas_call(
        functools.partial(sparse_kernel, base, stage),
        grid_spec=pltpu.PrefetchScalarGridSpec(
            num_scalar_prefetch=1, grid=(),
            in_specs=[pl.BlockSpec(memory_space=pl.ANY)] * 2,
            out_specs=[pl.BlockSpec(memory_space=pl.ANY)] * nout,
            scratch_shapes=[pltpu.VMEM((RING, size, GROUP * size), tiles.dtype), pltpu.VMEM((RING, GROUP * size, width), panels.dtype),
                            pltpu.VMEM((nout * rows + 1, size, width), jnp.float32),
                            pltpu.SemaphoreType.DMA((RING,)), pltpu.SemaphoreType.DMA((RING,)), pltpu.SemaphoreType.DMA((nout * rows,))]),
        out_shape=[jax.ShapeDtypeStruct((rows, size, width), jnp.float32)] * nout,
        compiler_params=pltpu.CompilerParams(vmem_limit_bytes=67_000_000),
        cost_estimate=pl.CostEstimate(flops=2 * 360 * 128 * 128 * 512 * rows * nout // 24, bytes_accessed=50_000_000 * rows * nout // 24, transcendentals=0),
        name="tile_sums",
    )(plan, tiles, panels)

HI = lax.Precision.HIGHEST

def dot_hi(a, b, dims):
    return lax.dot_general(a, b, (dims, ((), ())), precision=HI, preferred_element_type=jnp.float32)

def plan_kernel(ncol, chunk, count_ref, places_ref, plan_ref, wide):
    me = lax.axis_index("col")
    width = wide.shape[1]
    wide[...] = jnp.zeros_like(wide)
    wide[:, :places_ref.shape[1]] = places_ref[...]
    rows = wide[0:1, :]
    cols = wide[1:2, :]
    ids = lax.broadcasted_iota(jnp.int32, (1, width), 1)
    live = ids < count_ref[0, 0]
    dest = jnp.zeros_like(rows)
    for q in range(1, ncol):
        dest = dest + (rows >= q * chunk).astype(jnp.int32)
    sub = rows - dest * chunk
    step = jnp.where(sub < chunk // 2, (me + 2 * ncol - 1 - dest) & (ncol - 1), (dest + 2 * ncol - 1 - me) & (ncol - 1))
    place = step * chunk + sub
    shelf = lax.broadcasted_iota(jnp.int32, (32, width), 0)
    held = jnp.where(shelf == jnp.where(live, place, 99), 1.0, 0.0)
    before = lax.broadcasted_iota(jnp.int32, (width, width), 0) < lax.broadcasted_iota(jnp.int32, (width, width), 1)
    rank = jnp.dot(held.astype(jnp.bfloat16), jnp.where(before, 1.0, 0.0).astype(jnp.bfloat16), preferred_element_type=jnp.float32)
    groups = (jnp.sum(held, axis=1, keepdims=True).astype(jnp.int32) + GROUP - 1) // GROUP
    wide_groups = jnp.broadcast_to(groups.astype(jnp.float32), (32, 128))
    under = lax.broadcasted_iota(jnp.int32, (32, 32), 1) < lax.broadcasted_iota(jnp.int32, (32, 32), 0)
    ahead = jnp.dot(jnp.where(under, 1.0, 0.0).astype(jnp.bfloat16), wide_groups.astype(jnp.bfloat16), preferred_element_type=jnp.float32)
    spot = jnp.sum(held * (rank + GROUP * ahead[:, 0:1]), axis=0, keepdims=True).astype(jnp.int32)
    spot = jnp.where(live, spot, -1)
    word = (ids + cols * 512 + place * (1 << 18) + (1 << 23)).astype(jnp.float32)
    high = jnp.where(lax.broadcasted_iota(jnp.int32, (8, width), 0) == (spot >> 7), word, 0.0)
    low = jnp.where(lax.broadcasted_iota(jnp.int32, (128, width), 0) == (spot & 127), 1.0, 0.0)
    plan = dot_hi(high, low, ((1,), (1,))).astype(jnp.int32)
    r8 = lax.broadcasted_iota(jnp.int32, (8, 128), 0)
    c8 = lax.broadcasted_iota(jnp.int32, (8, 128), 1)
    shelf8 = lax.broadcasted_iota(jnp.int32, (32, 128), 0)
    n0 = jnp.sum(jnp.where(shelf8 < chunk, wide_groups, 0.0), axis=0, keepdims=True).astype(jnp.int32)
    n1 = jnp.sum(wide_groups, axis=0, keepdims=True).astype(jnp.int32)
    plan_ref[...] = jnp.where(r8 == 7, jnp.where(c8 == 1, n0, jnp.where(c8 == 2, n1, 0)), plan)

def make_plan(places, count, ncol, chunk_rows):
    width = -(-places.shape[1] // 128) * 128
    return pl.pallas_call(
        functools.partial(plan_kernel, ncol, chunk_rows),
        out_shape=jax.ShapeDtypeStruct((8, 128), jnp.int32),
        in_specs=[pl.BlockSpec(memory_space=pltpu.SMEM), pl.BlockSpec(memory_space=pltpu.VMEM)],
        out_specs=pl.BlockSpec(memory_space=pltpu.VMEM),
        scratch_shapes=[pltpu.VMEM((2, width), jnp.int32)],
        name="tile_plan",
    )(count, places).reshape(8 * 128)


MESH = pl.DeviceIdType.MESH
BLOCKS = (((0, 0), (2, 2), (0, 1), (2, 3), (0, 2)), ((1, 1), (3, 3), (1, 2), (0, 3), (1, 3)))
SPOT = {ij: (h, b) for h in range(2) for b, ij in enumerate(BLOCKS[h])}

def ring_kernel(dims, up_ref, down_ref, later_ref, rows_ref, out_ref,
                head, later, box1, box2, part, mate, mine, inbox, tower, full,
                hsem, lsem, osem, s1, r1, s2, r2, cs, cr, ps, pr, zs, zr, gs, gr, fs, fr):
    zn, xn, yn = dims
    row = lax.axis_index("row")
    y = lax.axis_index("col")
    core = lax.rem(row, 2)
    x = lax.rem(row // 2, xn)
    z = row // (2 * xn)
    other = 1 - core
    count = up_ref.shape[0]
    tall = up_ref.shape[1]

    def at(zz, xx, yy, cc):
        return ((zz * xn + xx) * 2 + cc, yy)

    partner = at(z, x, y, other)
    plane = []
    for j in range(1, xn * yn):
        dx, dy = j // yn, j % yn
        plane.append((at(z, lax.rem(x + dx, xn), lax.rem(y + dy, yn), core),
                      lax.rem(x + dx, xn) * yn + lax.rem(y + dy, yn),
                      lax.rem(x + xn - dx, xn) * yn + lax.rem(y + yn - dy, yn)))
    column = [at(lax.rem(z + j, zn), x, y, core) for j in range(1, zn)]
    own = x * yn + y
    piece = mine.shape[0] // (xn * yn)
    ring = [(row, lax.rem(y + 1, yn)), (row, lax.rem(y + yn - 1, yn))]

    barrier = pltpu.get_barrier_semaphore()
    peers = [partner] + [p[0] for p in plane] + column
    for peer in peers:
        pl.semaphore_signal(barrier, inc=1, device_id=peer, device_id_type=MESH)

    def remote(src, dst, send, recv, dev):
        return pltpu.make_async_remote_copy(src_ref=src, dst_ref=dst, send_sem=send, recv_sem=recv, device_id=dev, device_id_type=MESH)

    def head_copy(i, d):
        return pltpu.make_async_copy((up_ref, down_ref)[d].at[i], head.at[d, i], hsem.at[d, i])

    def later_copy(step, i, d):
        p = (2 * step + d) * count + i
        return pltpu.make_async_copy(later_ref.at[p], later.at[step, d, i], lsem.at[step, d, i])

    def row_copy(i, d):
        return pltpu.make_async_copy(box2.at[d, i], rows_ref.at[d, i], osem.at[d, i])

    def hop1(i, d):
        return remote(head.at[d, i], box1.at[d, i], s1.at[d, i], r1.at[d, i], ring[d])

    def hop2(i, d):
        return remote(box1.at[d, i], box2.at[d, i], s2.at[d, i], r2.at[d, i], ring[d])

    for i in range(count):
        for d in range(2):
            head_copy(i, d).start()
            later_copy(0, i, d).start()
    for step in range(1, 3):
        for i in range(count):
            for d in range(2):
                later_copy(step, i, d).start()
    part[...] = jnp.zeros_like(part)
    pl.semaphore_wait(barrier, len(peers))

    def first(i, c):
        for d in range(2):
            head_copy(i, d).wait()
            later_copy(0, i, d).wait()
            head[d, i] = head[d, i] + later[0, d, i]
            hop1(i, d).start()
        return c

    lax.fori_loop(0, count, first, 0)

    def second(i, c):
        for d in range(2):
            later_copy(1, i, d).wait()
            hop1(i, d).wait_recv()
            box1[d, i] = box1[d, i] + later[1, d, i]
            hop2(i, d).start()
        return c

    lax.fori_loop(0, count, second, 0)

    def third(i, c):
        for d in range(2):
            later_copy(2, i, d).wait()
            hop2(i, d).wait_recv()
            total = box2[d, i] + later[2, d, i]
            box2[d, i] = total
            row_copy(i, d).start()
            for a in range(4):
                got = dot_hi(total[:, 128 * a:128 * a + 128], total[:, 128 * a:], ((0,), (0,)))
                for j in range(a, 4):
                    h, b = SPOT[a, j]
                    part[h, 128 * b:128 * b + 128, :] = part[h, 128 * b:128 * b + 128, :] + got[:, 128 * (j - a):128 * (j - a) + 128]
        return c

    lax.fori_loop(0, count, third, 0)

    swap = remote(part.at[other], mate, cs, cr, partner)
    swap.start()
    swap.wait_recv()
    mine[...] = part[core] + mate[...]
    order = sorted(range(len(plane)), key=lambda j: -(min((j + 1) // yn, xn - (j + 1) // yn) + min((j + 1) % yn, yn - (j + 1) % yn)))
    scatter = []
    for j in order:
        dev, theirs, _ = plane[j]
        c = remote(mine.at[pl.ds(pl.multiple_of(theirs * piece, 8), piece)], inbox.at[j], ps.at[j], pr.at[j], dev)
        c.start()
        scatter.append(c)
    total = mine[pl.ds(pl.multiple_of(own * piece, 8), piece), :]
    for j, c in zip(reversed(order), reversed(scatter)):
        c.wait_recv()
        total = total + inbox[j]
    tower[z] = total
    climb = []
    for j in sorted(range(zn - 1), key=lambda j: -min(j + 1, zn - j - 1)):
        c = remote(tower.at[z], tower.at[z], zs.at[j], zr.at[j], column[j])
        c.start()
        climb.append(c)
    for c in climb:
        c.wait_recv()
    total = tower[0]
    for k in range(1, zn):
        total = total + tower[k]
    full[core, own] = total
    spread = {}
    for j in order:
        dev, _, _ = plane[j]
        spread[j] = remote(full.at[core, own], full.at[core, own], gs.at[j], gr.at[j], dev)
        spread[j].start()
    hand = [remote(full.at[core, own], full.at[core, own], fs.at[len(plane)], fr.at[len(plane)], partner)]
    hand[0].start()
    for j in reversed(order):
        spread[j].wait_recv()
        source = plane[j][2]
        c = remote(full.at[core, source], full.at[core, source], fs.at[j], fr.at[j], partner)
        c.start()
        hand.append(c)
    for c in hand:
        c.wait_recv()
    out_ref[...] = full[...]
    for c in [swap] + scatter + climb + list(spread.values()) + hand:
        c.wait_send()

    def drain(i, c):
        for d in range(2):
            hop1(i, d).wait_send()
            hop2(i, d).wait_send()
            row_copy(i, d).wait()
        return c

    lax.fori_loop(0, count, drain, 0)

def ring_sum(up, down, later, dims):
    zn, xn, yn = dims
    count, tall, n = up.shape
    pieces = xn * yn
    deep = 5 * 128
    sem = pltpu.SemaphoreType.DMA
    f32 = jnp.float32
    return pl.pallas_call(
        functools.partial(ring_kernel, dims),
        out_shape=(jax.ShapeDtypeStruct((2, count, tall, n), f32), jax.ShapeDtypeStruct((2, pieces, deep // pieces, 128), f32)),
        in_specs=[pl.BlockSpec(memory_space=pl.ANY)] * 3,
        out_specs=(pl.BlockSpec(memory_space=pl.ANY), pl.BlockSpec(memory_space=pltpu.VMEM)),
        scratch_shapes=[pltpu.VMEM((2, count, tall, n), f32), pltpu.VMEM((3, 2, count, tall, n), f32),
                        pltpu.VMEM((2, count, tall, n), f32), pltpu.VMEM((2, count, tall, n), f32),
                        pltpu.VMEM((2, deep, 128), f32), pltpu.VMEM((deep, 128), f32), pltpu.VMEM((deep, 128), f32),
                        pltpu.VMEM((pieces - 1, deep // pieces, 128), f32), pltpu.VMEM((zn, deep // pieces, 128), f32),
                        pltpu.VMEM((2, pieces, deep // pieces, 128), f32),
                        sem((2, count)), sem((3, 2, count)), sem((2, count)), sem((2, count)), sem((2, count)), sem((2, count)), sem((2, count)),
                        sem, sem, sem((pieces - 1,)), sem((pieces - 1,)), sem((zn - 1,)), sem((zn - 1,)),
                        sem((pieces - 1,)), sem((pieces - 1,)), sem((pieces,)), sem((pieces,))],
        compiler_params=pltpu.CompilerParams(collective_id=0, has_side_effects=True, vmem_limit_bytes=67_000_000),
        name="ring_sum",
    )(up, down, later)


def factor_block(a_ref, w_ref, u_ref, c_ref):
    n = 128
    nv = n // 8
    lane = lax.broadcasted_iota(jnp.int32, (8, n), 1)
    sub = lax.broadcasted_iota(jnp.int32, (8, n), 0)
    a = [a_ref[8 * v:8 * v + 8, :] for v in range(nv)]
    b = [jnp.where(lane == sub + 8 * v, 1.0, 0.0).astype(jnp.float32) for v in range(nv)]
    for r in range(nv):
        col = {}
        for v in range(r, nv):
            for k in range(8):
                col[k, v] = jnp.broadcast_to(a[v][:, 8 * r + k:8 * r + k + 1], (8, n))
        for k in range(8):
            c_ref[r, 8 * k:8 * k + 8, :] = col[k, r]
        e = {}
        for k in range(8):
            for j in range(k, 8):
                e[k, j] = c_ref[r, pl.ds(8 * j + k, 8, stride=0), :]
        c_ref[r, 64:72, :] = a[r]
        c_ref[r, 72:80, :] = b[r]
        ra = [c_ref[r, pl.ds(64 + k, 8, stride=0), :] for k in range(8)]
        rb = [c_ref[r, pl.ds(72 + k, 8, stride=0), :] for k in range(8)]
        for k in range(8):
            rs = lax.rsqrt(e[k, k])
            for j in range(k + 1, 8):
                e[k, j] = e[k, j] * rs
            for i in range(k + 1, 8):
                for j in range(i, 8):
                    e[i, j] = e[i, j] - e[k, i] * e[k, j]
            ra[k] = ra[k] * rs
            rb[k] = rb[k] * rs
            for j in range(k + 1, 8):
                ra[j] = ra[j] - e[k, j] * ra[k]
                rb[j] = rb[j] - e[k, j] * rb[k]
            for v in range(r + 1, nv):
                col[k, v] = col[k, v] * rs
                for j in range(k + 1, 8):
                    col[j, v] = col[j, v] - e[k, j] * col[k, v]
                a[v] = a[v] - col[k, v] * ra[k]
                b[v] = b[v] - col[k, v] * rb[k]
        ua, ub = ra[0], rb[0]
        for k in range(1, 8):
            ua = jnp.where(sub == k, ra[k], ua)
            ub = jnp.where(sub == k, rb[k], ub)
        u_ref[8 * r:8 * r + 8, :] = jnp.where(lane >= sub + 8 * r, ua, 0.0)
        w_ref[8 * r:8 * r + 8, :] = ub

def chol_kernel(scale, g_ref, s_ref, x_ref, t_ref, gw, xs, d_ref, w_ref, u_ref, c_ref):
    n = gw.shape[0]
    nb = n // 128
    for h in range(2):
        for b, (i, j) in enumerate(BLOCKS[h]):
            gw[128 * i:128 * i + 128, 128 * j:128 * j + 128] = g_ref[h, b]
    xs[...] = s_ref[...] * scale
    t_ref[...] = jnp.zeros_like(t_ref)
    for k in range(nb):
        lo = 128 * k
        hi = lo + 128
        d_ref[...] = gw[lo:hi, lo:hi]
        factor_block(d_ref, w_ref, u_ref, c_ref)
        w = w_ref[...]
        t_ref[lo:hi, lo:hi] = u_ref[...] * (1.0 / scale)
        if hi < n:
            up = dot_hi(w, gw[lo:hi, hi:n], ((1,), (0,)))
            t_ref[lo:hi, hi:n] = up * (1.0 / scale)
            for i in range(hi, n, 128):
                gw[i:i + 128, i:n] = gw[i:i + 128, i:n] - dot_hi(up[:, i - hi:i - hi + 128], up[:, i - hi:], ((0,), (0,)))
        xk = dot_hi(xs[:, lo:hi], w, ((1,), (1,)))
        x_ref[:, lo:hi] = xk
        if hi < n:
            xs[:, hi:n] = xs[:, hi:n] - dot_hi(xk, up, ((1,), (0,)))


def chol_solve(gram, rows, scale):
    m, n = rows.shape
    return pl.pallas_call(
        functools.partial(chol_kernel, scale),
        out_shape=(jax.ShapeDtypeStruct((m, n), jnp.float32), jax.ShapeDtypeStruct((n, n), jnp.float32)),
        in_specs=[pl.BlockSpec(memory_space=pltpu.VMEM)] * 2,
        out_specs=(pl.BlockSpec(memory_space=pltpu.VMEM),) * 2,
        scratch_shapes=[pltpu.VMEM((n, n), jnp.float32), pltpu.VMEM((m, n), jnp.float32),
                        pltpu.VMEM((128, 128), jnp.float32), pltpu.VMEM((128, 128), jnp.float32),
                        pltpu.VMEM((128, 128), jnp.float32), pltpu.VMEM((16, 80, 128), jnp.float32)],
        name="factor_solve",
    )(gram, rows)


def shifted(block, distance):
    count = lax.axis_size("col")
    return lax.ppermute(block, "col", [(i, (i + distance) % count) for i in range(count)])


def body(tile_values, tile_places, tile_counts, sketch):
    tile_stack = tile_values[0, 0]
    tile_size = tile_stack.shape[1]
    sketch_width = sketch.shape[1]
    row_devices = lax.axis_size("row")
    col_devices = lax.axis_size("col")
    local_rows = sketch.shape[0] // row_devices
    chunk_rows = local_rows // tile_size
    half = chunk_rows // 2
    panels = sketch.reshape(-1, tile_size, sketch_width)
    plan = make_plan(tile_places[0, 0], tile_counts, col_devices, chunk_rows)
    up, down = sparse_sum(plan, 0, tile_stack, panels, 0, (2, half))
    (later,) = sparse_sum(plan, 1, tile_stack, panels, chunk_rows, (1, chunk_rows * (col_devices - 1)))
    own, gram = ring_sum(shifted(up, 1), shifted(down, -1), later, (row_devices // 8, 4, col_devices))
    own_rows = own.reshape(local_rows, sketch_width)
    gram_blocks = gram.reshape(2, 5, 128, 128)
    order_scale = math.sqrt(local_rows * row_devices * col_devices)
    basis_rows, upper = chol_solve(gram_blocks, own_rows, order_scale)
    return basis_rows, upper


def solution(mesh):
    in_specs = (
        P("row", "col", None, None, None),
        P("row", "col", None, None),
        P("row", "col"),
        P("col", None),
    )
    out_specs = (P(("row", "col"), None), P())
    return jax.shard_map(body, mesh=mesh, in_specs=in_specs, out_specs=out_specs, check_vma=False)
```
